512 devices in a mesh: cube: 512 (over y, x, z, core).
Axes of the slice: x: 4, y: 4, z: 16, core: 2. Of those that a mesh axis runs over, the one named last changes fastest.
Arguments:
- offsets: float32 [3, 2097152], P(None, 'cube'), may hold values from 0 to 1
- charges: float32 [16, 2097152], P(None, 'cube'), may hold values from -6 to 6
- counts: int32 [16384], P('cube'), may hold values from 1 to 128, as said below
- u_list: int32 [16384, 27], P('cube'), may hold values from 0 to 16383, as said below
- v_src: int32 [16384, 32], P('cube'), may hold values from 0 to 175, as said below
- v_type: int32 [16384, 32], P('cube'), may hold values from 0 to 15
- wanted: int32 [512, 9, 16], P('cube'), may hold values from 0 to 31, as said below
- m2l: float32 [152, 2432], replicated, may hold values from -0.078125 to 0.078125
- uc2e: float32 [152, 152], replicated, may hold values from -0.5 to 0.5
- dc2e: float32 [152, 152], replicated, may hold values from -0.5 to 0.5
Outputs:
- potential: float32 [16, 2097152], P(None, 'cube')
The draws below stay inside these ranges and needn't reach their ends.
Inputs may be any that keep to these rules, and one draw needn't show every extreme that they name: `counts`: every leaf has at least one live point; the first leaf of each device is full. `u_list`: entry 0 of each row is the leaf itself; every entry lies within 8 leaves of the leaf in the global order. `v_src`: codes below 144 name hypercube dimension v // 16 and reader slot v % 16; larger codes name a leaf of the same device; entry 0 of each row is the leaf itself. `wanted`: entries of one list are distinct local leaf indices of the partner.
All inputs are finite; a program needn't handle non-finite values.
Results may differ from the reference program's by a relative error of at most 0.0003.
Values sent between devices are 32-bit elements; how exact they have to be, the bound alone decides.
A program may use at most 64 MiB of HBM per device.

```python
import math
import jax
import jax.numpy as jnp
import numpy as np
from jax import lax

LEAVES_DEV = 32
LEAF_PTS = 128
PROBES = 16
EQUIV = 152
TYPES = 16
U_SLOTS = 27
V_SLOTS = 32
GHOST = 8
READ_CAP = 16
DEVICE_COUNT = 512
BITS = 9
LEAVES = 16384
POINTS = 2097152
N_CUBE = 512


def draw_counts(key, part):
    drawn = jax.random.randint(key, (LEAVES,), 1, LEAF_PTS + 1)
    leading = jnp.arange(LEAVES, dtype=jnp.int32) % LEAVES_DEV == 0
    return jnp.where(leading, LEAF_PTS, drawn).astype(jnp.int32)


def draw_u_list(key, part):
    leaf_ids = jnp.arange(LEAVES, dtype=jnp.int32)[:, None]
    moved = jax.random.randint(key, (LEAVES, U_SLOTS), -GHOST, GHOST + 1)
    moved = moved.at[:, 0].set(0)
    return jnp.clip(leaf_ids + moved, 0, LEAVES - 1).astype(jnp.int32)


def draw_v_src(key, part):
    first_key, second_key, third_key = jax.random.split(key, 3)
    chosen_bit = jax.random.randint(first_key, (LEAVES, V_SLOTS), 0, BITS + 1)
    remote = chosen_bit * READ_CAP + jax.random.randint(second_key, (LEAVES, V_SLOTS), 0, READ_CAP)
    own_leaf = BITS * READ_CAP + jax.random.randint(third_key, (LEAVES, V_SLOTS), 0, LEAVES_DEV)
    values = jnp.where(chosen_bit < BITS, remote, own_leaf)
    itself = BITS * READ_CAP + jnp.arange(LEAVES, dtype=jnp.int32) % LEAVES_DEV
    values = values.at[:, 0].set(itself)
    return values.astype(jnp.int32)


def draw_wanted(key, part):
    scores = jax.random.randint(key, (DEVICE_COUNT, BITS, LEAVES_DEV), 0, 1 << 20)
    scores = scores * LEAVES_DEV + jnp.arange(LEAVES_DEV, dtype=jnp.int32)
    ranked = jnp.argsort(scores, axis=-1)
    return ranked[:, :, :READ_CAP].astype(jnp.int32)


def plant(values, rng, low, top_value):
    index_at = [jax.random.randint(jax.random.fold_in(rng, axis), (), 0, length) for axis, length in enumerate(values.shape)]
    widest = values.shape.index(max(values.shape))
    neighbour = index_at[:widest] + [(index_at[widest] + 1) % values.shape[widest]] + index_at[widest + 1:]
    return values.at[tuple(index_at)].set(low).at[tuple(neighbour)].set(top_value)


def block_scale(key, dims, cuts, smallest, largest):
    factor_of = 1.0
    for dim, blocks in cuts:
        steps = jax.random.uniform(jax.random.fold_in(jax.random.fold_in(key, 6), dim), (blocks,), jnp.float32, smallest / len(cuts), largest / len(cuts))
        factor_of = factor_of * jnp.repeat(jnp.exp(steps), dims[dim] // blocks).reshape((-1,) + (1,) * (len(dims) - 1 - dim))
    return factor_of


def bell_draw(stream_key, shape, deviation, limit, cuts=(), kind=jnp.bfloat16):
    values = deviation * jax.random.normal(stream_key, shape, jnp.float32)
    if cuts:
        values = values * block_scale(stream_key, shape, cuts, -0.22, 0.18)
    return jnp.clip(values, -limit, limit).astype(kind)


def setup_inputs(seed: int = 0) -> dict:
    key_of = jax.random.split(jax.random.key(seed), 11)
    return {
        "offsets": jnp.clip(1.0 * jax.random.uniform(key_of[0], (3, POINTS), jnp.float32) ** block_scale(key_of[0], (3, POINTS), ((1, 512),), -0.2, 0.2), 0.0, 1.0),
        "charges": bell_draw(key_of[1], (PROBES, POINTS), 1.0, 6.0, ((1, 512),), jnp.float32),
        "counts": draw_counts(jax.random.fold_in(key_of[10], 71), 0),
        "u_list": draw_u_list(jax.random.fold_in(key_of[10], 71), 0),
        "v_src": draw_v_src(jax.random.fold_in(key_of[10], 71), 0),
        "v_type": plant(jax.random.randint(key_of[5], (LEAVES, V_SLOTS), 0, TYPES), jax.random.fold_in(key_of[5], 1), 0, TYPES - 1).astype(jnp.int32),
        "wanted": draw_wanted(jax.random.fold_in(key_of[10], 71), 0),
        "m2l": bell_draw(key_of[7], (EQUIV, TYPES * EQUIV), (V_SLOTS * EQUIV) ** -0.5, 0.078125, (), jnp.float32),
        "uc2e": bell_draw(key_of[8], (EQUIV, EQUIV), EQUIV ** -0.5, 0.5, (), jnp.float32),
        "dc2e": bell_draw(key_of[9], (EQUIV, EQUIV), EQUIV ** -0.5, 0.5, (), jnp.float32),
    }


soften = 0.01
inv_four_pi = 1.0 / (4.0 * math.pi)
surface_radius = 0.55
highest = lax.Precision.HIGHEST

def surface_table():
    lattice = np.arange(6)
    coords = np.stack(np.meshgrid(lattice, lattice, lattice, indexing='ij'), 0).reshape(3, -1)
    coords = (coords - 2.5) / 2.5
    on_face = np.max(np.abs(coords), axis=0) > 0.99
    return coords[:, on_face].astype(np.float32)

def leaf_corner(leaf_ids):
    corners = []
    for axis_num in range(3):
        summed = jnp.zeros_like(leaf_ids)
        for digit_num in range(10):
            summed = summed + ((leaf_ids >> 3 * digit_num + axis_num & 1) << digit_num)
        corners.append(summed)
    return jnp.stack(corners, 0).astype(jnp.float32)

def kernel(targets, sources):
    squared = jnp.zeros((targets.shape[-1], sources.shape[-1]), jnp.float32)
    for axis_num in range(3):
        squared = squared + (targets[axis_num][:, None] - sources[axis_num][None, :]) ** 2
    return inv_four_pi * lax.rsqrt(squared + soften)

def upward(points, masked, centers, surface, uc2e):
    checks = centers[:, :, None] + surface_radius * surface[:, None, :]
    tiles = jax.vmap(kernel, in_axes=(1, 1))(checks, points)
    potent = jnp.einsum('ljp,qlp->lqj', tiles, masked, precision=highest)
    return jnp.einsum('lqj,ij->lqi', potent, uc2e, precision=highest)

def downward(points, centers, surface, downcheck, dc2e):
    downeq = jnp.einsum('lqi,ji->lqj', downcheck, dc2e, precision=highest)
    equivs = centers[:, :, None] + surface_radius * surface[:, None, :]
    tiles = jax.vmap(kernel, in_axes=(1, 1))(points, equivs)
    return jnp.einsum('lpj,lqj->qlp', tiles, downeq, precision=highest)

def near_field(targets, src_pts, src_chg):
    leaf_count = targets.shape[0]
    group = math.gcd(leaf_count, 8)
    blocks = leaf_count // group

    def one_group(packed):
        tgt, spt, sch = packed
        tiles = jax.vmap(kernel)(tgt, spt)
        return jnp.einsum('gpn,gqn->gqp', tiles, sch, precision=highest)
    result = lax.map(one_group, (targets.reshape(blocks, group, targets.shape[1], targets.shape[2]), src_pts.reshape(blocks, group, src_pts.shape[1], src_pts.shape[2]), src_chg.reshape(blocks, group, src_chg.shape[1], src_chg.shape[2])))
    return result.reshape(leaf_count, src_chg.shape[1], targets.shape[2])

def reference(offsets, charges, counts, u_list, v_src, v_type, wanted, m2l, uc2e, dc2e):
    total = counts.shape[0]
    surface = jnp.asarray(surface_table())
    m2l_ops = m2l.reshape(EQUIV, TYPES, EQUIV)
    inside = (jnp.arange(LEAF_PTS, dtype=jnp.int32)[None, :] < counts[:, None]).astype(jnp.float32)
    leaf_ids = jnp.arange(total, dtype=jnp.int32)
    corners = leaf_corner(leaf_ids)
    centers = corners + 0.5
    points = offsets.reshape(3, total, LEAF_PTS) + corners[:, :, None]
    masked = charges.reshape(PROBES, total, LEAF_PTS) * inside[None]

    def up_device(device):
        start = (device * LEAVES_DEV).astype(jnp.int32)
        pts = lax.dynamic_slice_in_dim(points, start, LEAVES_DEV, 1)
        chg = lax.dynamic_slice_in_dim(masked, start, LEAVES_DEV, 1)
        ctr = lax.dynamic_slice_in_dim(centers, start, LEAVES_DEV, 1)
        return upward(pts, chg, ctr, surface, uc2e)
    devices = jnp.arange(N_CUBE, dtype=jnp.int32)
    up_all = lax.map(up_device, devices).reshape(total, PROBES, EQUIV)
    onehot_types = jnp.arange(TYPES, dtype=jnp.int32)

    def out_device(device):
        start = (device * LEAVES_DEV).astype(jnp.int32)
        pts = lax.dynamic_slice_in_dim(points, start, LEAVES_DEV, 1)
        ctr = lax.dynamic_slice_in_dim(centers, start, LEAVES_DEV, 1)
        live = lax.dynamic_slice_in_dim(inside, start, LEAVES_DEV, 0)
        codes = lax.dynamic_slice_in_dim(v_src, start, LEAVES_DEV, 0)
        kinds = lax.dynamic_slice_in_dim(v_type, start, LEAVES_DEV, 0)
        near_ids = lax.dynamic_slice_in_dim(u_list, start, LEAVES_DEV, 0)
        bit_part = jnp.minimum(codes // READ_CAP, BITS - 1)
        slot_part = codes % READ_CAP
        remote_leaf = wanted[device][bit_part, slot_part]
        partner = jnp.bitwise_xor(device, jnp.left_shift(jnp.int32(1), bit_part))
        sources = jnp.where(codes >= BITS * READ_CAP, start + codes - BITS * READ_CAP, partner * LEAVES_DEV + remote_leaf).astype(jnp.int32)
        gathered = up_all[sources]
        onehot = (kinds[:, :, None] == onehot_types[None, None, :]).astype(jnp.float32)
        by_type = jnp.einsum('lvt,lvqj->ltqj', onehot, gathered, precision=highest)
        downcheck = jnp.einsum('ltqj,itj->lqi', by_type, m2l_ops, precision=highest)
        far = downward(pts, ctr, surface, downcheck, dc2e)
        src_pts = points[:, near_ids].transpose(1, 0, 2, 3).reshape(LEAVES_DEV, 3, U_SLOTS * LEAF_PTS)
        src_chg = masked[:, near_ids].transpose(1, 0, 2, 3).reshape(LEAVES_DEV, PROBES, U_SLOTS * LEAF_PTS)
        near = near_field(pts.transpose(1, 0, 2), src_pts, src_chg).transpose(1, 0, 2)
        return (near + far) * live[None]
    result = lax.map(out_device, devices)
    return result.transpose(1, 0, 2, 3).reshape(PROBES, total * LEAF_PTS)
```

```python
import math

import jax
import jax.numpy as jnp
import numpy as np
from jax import lax
from jax.experimental import pallas as pl
from jax.experimental.pallas import tpu as pltpu
from jax.sharding import PartitionSpec as P

GHOST = 8
SOFTEN = 0.01
INV_FOUR_PI = 1.0 / (4.0 * math.pi)
SURFACE_RADIUS = 0.55

LEAVES = 32
PTS = 128
PROBES = 16
EQUIV = 152
TYPES = 16
U_SLOTS = 27
V_SLOTS = 32
CAP = 16
EXT = LEAVES + 2 * GHOST
REACH = 2 * GHOST + 1
CHUNKS = 2
QC = PROBES // CHUNKS
REM = EQUIV - 128
CW = QC * 128 + QC * 32
KW = TYPES * 128 + TYPES * 32
MESH = pl.DeviceIdType.MESH
f32, bf16 = jnp.float32, jnp.bfloat16


def surface_table():
    lattice = np.arange(6)
    coords = np.stack(np.meshgrid(lattice, lattice, lattice, indexing="ij"), 0).reshape(3, -1)
    coords = (coords - 2.5) / 2.5
    on_face = np.max(np.abs(coords), axis=0) > 0.99
    return coords[:, on_face].astype(np.float32)


def dot_nt(a, b):
    return lax.dot_general(a, b, (((1,), (1,)), ((), ())), preferred_element_type=f32)


def dot_nn(a, b):
    return lax.dot_general(a, b, (((1,), (0,)), ((), ())), preferred_element_type=f32)


def split(x):
    high = x.astype(bf16)
    return high, (x - high.astype(f32)).astype(bf16)


def split3(x):
    first = x.astype(bf16).astype(f32)
    rest = x - first
    second = rest.astype(bf16).astype(f32)
    return first, second, rest - second


def iota(shape, dim):
    return lax.broadcasted_iota(jnp.int32, shape, dim)


def source_rows(x):
    row = iota(x.shape, 0)
    x = jnp.where(row < 3, x, 0.0)
    norm = jnp.sum(x * x, axis=0, keepdims=True) + SOFTEN
    e = jnp.where(row == 3, norm, jnp.where(row == 4, 1.0, x))
    a, b, c = split3(e)
    return jnp.concatenate([a, b, a, c, a, b], axis=0)


def target_rows(x):
    row = iota(x.shape, 0)
    x = jnp.where(row < 3, x, 0.0)
    norm = jnp.sum(x * x, axis=0, keepdims=True)
    e = jnp.where(row == 3, 1.0, jnp.where(row == 4, norm, -2.0 * x))
    a, b, c = split3(e)
    return jnp.concatenate([a, a, b, a, c, b], axis=0)


def column(row_vec, n, shift):
    m = row_vec.shape[1]
    wide = jnp.broadcast_to(row_vec.astype(f32), (n, m))
    hit = iota((n, m), 1) == iota((n, m), 0) + shift
    return jnp.sum(jnp.where(hit, wide, 0.0), axis=1, keepdims=True)


def lanes(i, width=128):
    return pl.ds(pl.multiple_of(i * width, width), width)


def make_kernel(bits, count):
    rows = bits * CAP + LEAVES

    def kern(off, chg, cnt, ulist, vsrc, vtype, wanted, m2l, uc, dc, surf, out,
             c3, pts, mq, cntb, mult, fs, kh_s, kl_s, chk, up, ups, stage, got, tlf, tl,
             mh, ml, lmh, lml, near, dq, uch, ucl, dch, dcl, hoff, hchg, hcnt, wrecv,
             w_ss, w_rs, h_ss, h_rs, d_ss, d_rs):
        me = lax.axis_index("cube")
        first = me * LEAVES
        partners = [jnp.bitwise_xor(me, 1 << b) for b in range(bits)]
        nxt = lax.rem(me + 1, count)
        prv = lax.rem(me + count - 1, count)

        barrier = pltpu.get_barrier_semaphore()
        for other in partners + [nxt, prv]:
            pl.semaphore_signal(barrier, inc=1, device_id=(other,), device_id_type=MESH)

        ids = first - GHOST + iota((EXT, 8, 128), 0)
        axis = iota((EXT, 8, 128), 1)
        corner = jnp.zeros((EXT, 8, 128), jnp.int32)
        for digit in range(5):
            corner = corner + ((lax.shift_right_arithmetic(ids, axis + 3 * digit) & 1) << digit)
        c3[...] = jnp.where(axis < 3, corner, 0).astype(f32)
        lane = iota((PROBES, PTS), 1).astype(f32)
        pts[...] = jnp.zeros((EXT, 8, 128), f32)
        cntb[GHOST:GHOST + LEAVES, :] = jnp.broadcast_to(column(cnt[...], LEAVES, 0), (LEAVES, 128))

        def place(h, position, charge):
            pts[h, 0:3, :] = position + c3[h, 0:3, :]
            live = lane < cntb[pl.ds(h, 1), :]
            mq[h] = jnp.where(live, charge, 0.0) * INV_FOUR_PI

        def own_leaf(l, carry):
            place(l + GHOST, off[:, lanes(l)], chg[:, lanes(l)])
            return carry

        lax.fori_loop(0, LEAVES, own_leaf, 0)

        uch[...] = jnp.zeros(uch.shape, bf16)
        ucl[...] = jnp.zeros(ucl.shape, bf16)
        u_h, u_l = split(uc[...])
        uch[0:128, 0:EQUIV] = u_h[0:128]
        ucl[0:128, 0:EQUIV] = u_l[0:128]
        for g in range(4):
            uch[128 + 32 * g:128 + 32 * g + REM, 0:EQUIV] = u_h[128:EQUIV]
            ucl[128 + 32 * g:128 + 32 * g + REM, 0:EQUIV] = u_l[128:EQUIV]
        surf_rows = source_rows(surf[...]).astype(bf16)

        def upward(l, carry):
            h = l + GHOST
            local = pts[h] - (c3[h] + 0.5)
            rows_t = jnp.transpose(target_rows(local)).astype(bf16)
            tile = lax.rsqrt(dot_nn(rows_t, surf_rows))
            k_h, k_l = split(tile)
            kh_s[l] = k_h
            kl_s[l] = k_l
            q_h, q_l = split(mq[h])
            both = dot_nn(jnp.concatenate([q_h, q_l], 0), k_h)
            check = both[:PROBES] + both[PROBES:] + dot_nn(q_h, k_l)
            chk[0, pl.ds(l, PROBES, stride=LEAVES), :] = check[:, :128]
            chk[1, pl.ds(l, PROBES, stride=LEAVES), :] = check[:, 128:]
            return carry

        lax.fori_loop(0, LEAVES, upward, 0)
        c_h, c_l = split(jnp.concatenate([chk[0], chk[1]], 1))
        dens = dot_nt(c_h, uch[...]) + dot_nt(c_l, uch[...]) + dot_nt(c_h, ucl[...])
        group_of = iota((LEAVES, 128), 1) // 32
        for q in range(PROBES):
            c, qq = q // QC, q % QC
            up[c, :, qq * 128:(qq + 1) * 128] = dens[q * LEAVES:(q + 1) * LEAVES, :128]
        for k in range(PROBES // 4):
            c, kk = (4 * k) // QC, k % (QC // 4)
            total = jnp.zeros((LEAVES, 128), f32)
            for g in range(4):
                q = 4 * k + g
                total = jnp.where(group_of == g, dens[q * LEAVES:(q + 1) * LEAVES, 128:], total)
            up[c, :, QC * 128 + kk * 128:QC * 128 + (kk + 1) * 128] = total
        for c in range(CHUNKS):
            value = up[c]
            got[c, bits * CAP:rows, :] = value
            a, b, d = split3(value)
            ups[c] = jnp.concatenate([a, b, d], 0).astype(bf16)

        pl.semaphore_wait(barrier, bits + 2)
        wants = []
        for b in range(bits):
            wants.append(pltpu.make_async_remote_copy(
                src_ref=wanted, dst_ref=wrecv.at[b], send_sem=w_ss.at[b], recv_sem=w_rs.at[b],
                device_id=(partners[b],), device_id_type=MESH))
            wants[-1].start()
        halos = []
        width = GHOST * PTS
        for side, other, begin in ((0, nxt, LEAVES * PTS - width), (1, prv, 0)):
            for k, (src, dst) in enumerate((
                    (off.at[:, pl.ds(begin, width)], hoff.at[side]),
                    (chg.at[:, pl.ds(begin, width)], hchg.at[side]),
                    (cnt, hcnt.at[side]))):
                halos.append(pltpu.make_async_remote_copy(
                    src_ref=src, dst_ref=dst, send_sem=h_ss.at[side, k], recv_sem=h_rs.at[side, k],
                    device_id=(other,), device_id_type=MESH))
                halos[-1].start()

        rel = ulist[...] - (first - GHOST) - iota((LEAVES, U_SLOTS), 0)
        for o in range(REACH):
            hits = jnp.sum(jnp.where(rel == o, 1.0, 0.0), axis=1, keepdims=True)
            mult[o] = jnp.broadcast_to(hits, (LEAVES, 128))

        def tally(l, carry):
            kinds = jnp.broadcast_to(vtype[pl.ds(l, 1), :], (TYPES, V_SLOTS))
            codes = jnp.broadcast_to(vsrc[pl.ds(l, 1), :], (256, V_SLOTS))
            of_kind = jnp.where(kinds == iota((TYPES, V_SLOTS), 0), 1.0, 0.0).astype(bf16)
            of_code = jnp.where(codes == iota((256, V_SLOTS), 0), 1.0, 0.0).astype(bf16)
            found = dot_nt(of_kind, of_code)
            tlf[0, pl.ds(l, TYPES, stride=LEAVES), :] = found[:, :128]
            tlf[1, pl.ds(l, TYPES, stride=LEAVES), :] = found[:, 128:]
            return carry

        lax.fori_loop(0, LEAVES, tally, 0)
        tl[...] = jnp.concatenate([tlf[0], tlf[1]], 1)[:, :rows].astype(bf16)

        for t in range(TYPES):
            a, b = split(m2l[:, t * EQUIV:t * EQUIV + 128])
            mh[:, t * 128:(t + 1) * 128] = a
            ml[:, t * 128:(t + 1) * 128] = b
        lane_m = iota((EQUIV, 128), 1)
        for tt in range(TYPES // 4):
            total = jnp.zeros((EQUIV, 128), f32)
            for g in range(4):
                t = 4 * tt + g
                tail = pltpu.roll(m2l[:, t * EQUIV + REM:(t + 1) * EQUIV],
                                  (32 * g + REM - 128) % 128, 1)
                inside = (lane_m >= 32 * g) & (lane_m < 32 * g + REM)
                total = jnp.where(inside, tail, total)
            a, b = split(total)
            mh[:, TYPES * 128 + tt * 128:TYPES * 128 + (tt + 1) * 128] = a
            ml[:, TYPES * 128 + tt * 128:TYPES * 128 + (tt + 1) * 128] = b
        dch[...] = jnp.zeros(dch.shape, bf16)
        dcl[...] = jnp.zeros(dcl.shape, bf16)
        d_h, d_l = split(dc[...] * INV_FOUR_PI)
        dch[0:EQUIV, :] = d_h
        dcl[0:EQUIV, :] = d_l

        for copy in wants:
            copy.wait()
        picks = []
        for b in range(bits):
            listed = column(wrecv[b, b:b + 1, :], CAP, 0)
            slot = (iota((CAP, 3 * LEAVES), 1) % LEAVES).astype(f32)
            picks.append(jnp.where(listed == slot, 1.0, 0.0))
        pick = jnp.concatenate(picks, 0).astype(bf16)
        sends = [[None] * bits for _ in range(CHUNKS)]
        order = [b for b in (4, 3, 2, 1, 6, 8, 5, 7, 0) if b < bits]
        for c in range(CHUNKS):
            stage[c] = dot_nn(pick, ups[c])
            for b in order:
                sends[c][b] = pltpu.make_async_remote_copy(
                    src_ref=stage.at[c, pl.ds(b * CAP, CAP)], dst_ref=got.at[c, pl.ds(b * CAP, CAP)],
                    send_sem=d_ss.at[c, b], recv_sem=d_rs.at[c, b],
                    device_id=(partners[b],), device_id_type=MESH)
                sends[c][b].start()

        def near_step(i, carry):
            l = lax.rem(i + GHOST, LEAVES)
            base = (l // 8) * 8
            middle = c3[base + GHOST] + 1.0

            @pl.when(i == 2 * GHOST)
            def _():
                for copy in halos:
                    copy.wait()
                cntb[0:GHOST, :] = jnp.broadcast_to(column(hcnt[0], GHOST, LEAVES - GHOST), (GHOST, 128))
                cntb[LEAVES + GHOST:EXT, :] = jnp.broadcast_to(column(hcnt[1], GHOST, 0), (GHOST, 128))
                for side, h0 in ((0, 0), (1, LEAVES + GHOST)):
                    for k in range(GHOST):
                        place(h0 + k, hoff[side, :, k * PTS:(k + 1) * PTS],
                              hchg[side, :, k * PTS:(k + 1) * PTS])

            @pl.when(lax.rem(i, 8) == 0)
            def _():
                for k in range(8 + 2 * GHOST):
                    fs[k] = source_rows(pts[base + k] - middle).astype(bf16)

            rows_t = jnp.transpose(target_rows(pts[l + GHOST] - middle)).astype(bf16)
            acc = jnp.zeros((2 * PROBES, PTS), f32)
            acc_l = jnp.zeros((PROBES, PTS), f32)
            for o in range(0, REACH, 2):
                both = [o, o + 1] if o + 1 < REACH else [o]
                src = jnp.concatenate([fs[l - base + k] for k in both], 1)
                k_h, k_l = split(lax.rsqrt(dot_nn(rows_t, src)))
                weighted = jnp.concatenate([mq[l + k] * mult[k, pl.ds(l, 1), :] for k in both], 1)
                w_h, w_l = split(weighted)
                acc = acc + dot_nt(jnp.concatenate([w_h, w_l], 0), k_h)
                acc_l = acc_l + dot_nt(w_h, k_l)
            near[:, lanes(l)] = acc[:PROBES] + acc[PROBES:] + acc_l
            return carry

        lax.fori_loop(0, LEAVES, near_step, 0)

        lane_g = iota((LEAVES, 128), 1) // 32
        for c in range(CHUNKS):
            for b in order:
                sends[c][b].wait()
            tallied = tl[...]
            for n in range(CW // 256):
                g_h, g_l = split(got[c, :, n * 256:(n + 1) * 256])
                by = dot_nn(tallied, g_h) + dot_nn(tallied, g_l)
                if n < QC // 2:
                    b_h, b_l = split(by)
                    for t in range(TYPES):
                        for k in range(2):
                            qq = 2 * n + k
                            r = slice(qq * LEAVES, (qq + 1) * LEAVES)
                            s = slice(t * 128, (t + 1) * 128)
                            lmh[r, s] = b_h[t * LEAVES:(t + 1) * LEAVES, k * 128:(k + 1) * 128]
                            lml[r, s] = b_l[t * LEAVES:(t + 1) * LEAVES, k * 128:(k + 1) * 128]
                else:
                    for k in range(2):
                        kk = 2 * (n - QC // 2) + k
                        for g in range(4):
                            qq = 4 * kk + g
                            for tt in range(TYPES // 4):
                                total = jnp.zeros((LEAVES, 128), f32)
                                for j in range(4):
                                    t = 4 * tt + j
                                    part = by[t * LEAVES:(t + 1) * LEAVES, k * 128:(k + 1) * 128]
                                    turn = (32 * (j - g)) % 128
                                    if turn:
                                        part = pltpu.roll(part, turn, 1)
                                    total = jnp.where(lane_g == j, part, total)
                                b_h, b_l = split(total)
                                r = slice(qq * LEAVES, (qq + 1) * LEAVES)
                                s = slice(TYPES * 128 + tt * 128, TYPES * 128 + (tt + 1) * 128)
                                lmh[r, s] = b_h
                                lml[r, s] = b_l
            down = (dot_nt(lmh[...], mh[...]) + dot_nt(lmh[...], ml[...]) + dot_nt(lml[...], mh[...]))
            w_h, w_l = split(down)
            eq = dot_nt(w_h, dch[...]) + dot_nt(w_l, dch[...]) + dot_nt(w_h, dcl[...])
            dq[0] = eq[:, :128]
            dq[1] = eq[:, 128:]

            def far(l, carry):
                e = jnp.concatenate([dq[0, pl.ds(l, QC, stride=LEAVES), :],
                                     dq[1, pl.ds(l, QC, stride=LEAVES), :]], 1)
                high = e.astype(bf16).astype(f32)
                pair = jnp.concatenate([high, e - high], 0).astype(bf16)
                part = dot_nt(pair, kh_s[l])
                part_l = dot_nt(pair, kl_s[l])
                value = part[:QC] + part[QC:] + part_l[:QC]
                live = iota((QC, PTS), 1).astype(f32) < cntb[pl.ds(l + GHOST, 1), :]
                out[c * QC:(c + 1) * QC, lanes(l)] = jnp.where(
                    live, near[c * QC:(c + 1) * QC, lanes(l)] + value, 0.0)
                return carry

            lax.fori_loop(0, LEAVES, far, 0, unroll=4)

    scratch = [
        pltpu.VMEM((EXT, 8, 128), f32),
        pltpu.VMEM((EXT, 8, 128), f32),
        pltpu.VMEM((EXT, PROBES, PTS), f32),
        pltpu.VMEM((EXT, 128), f32),
        pltpu.VMEM((REACH, LEAVES, 128), f32),
        pltpu.VMEM((8 + 2 * GHOST, 48, 128), bf16),
        pltpu.VMEM((LEAVES, PTS, 256), bf16),
        pltpu.VMEM((LEAVES, PTS, 256), bf16),
        pltpu.VMEM((2, PROBES * LEAVES, 128), f32),
        pltpu.VMEM((CHUNKS, LEAVES, CW), f32),
        pltpu.VMEM((CHUNKS, 3 * LEAVES, CW), bf16),
        pltpu.VMEM((CHUNKS, bits * CAP, CW), f32),
        pltpu.VMEM((CHUNKS, rows, CW), f32),
        pltpu.VMEM((2, TYPES * LEAVES, 128), f32),
        pltpu.VMEM((TYPES * LEAVES, rows), bf16),
        pltpu.VMEM((EQUIV, KW), bf16),
        pltpu.VMEM((EQUIV, KW), bf16),
        pltpu.VMEM((QC * LEAVES, KW), bf16),
        pltpu.VMEM((QC * LEAVES, KW), bf16),
        pltpu.VMEM((PROBES, LEAVES * PTS), f32),
        pltpu.VMEM((2, QC * LEAVES, 128), f32),
        pltpu.VMEM((256, 256), bf16),
        pltpu.VMEM((256, 256), bf16),
        pltpu.VMEM((256, EQUIV), bf16),
        pltpu.VMEM((256, EQUIV), bf16),
        pltpu.VMEM((2, 3, GHOST * PTS), f32),
        pltpu.VMEM((2, PROBES, GHOST * PTS), f32),
        pltpu.VMEM((2, 1, LEAVES), jnp.int32),
        pltpu.VMEM((bits, bits, CAP), jnp.int32),
        pltpu.SemaphoreType.DMA((bits,)),
        pltpu.SemaphoreType.DMA((bits,)),
        pltpu.SemaphoreType.DMA((2, 3)),
        pltpu.SemaphoreType.DMA((2, 3)),
        pltpu.SemaphoreType.DMA((CHUNKS, bits)),
        pltpu.SemaphoreType.DMA((CHUNKS, bits)),
    ]
    return kern, scratch


def shards(offsets, charges, counts, u_list, v_src, v_type, wanted, m2l, uc2e, dc2e):
    count = lax.axis_size("cube")
    bits = count.bit_length() - 1
    surface = np.zeros((8, 256), np.float32)
    surface[:3, :EQUIV] = np.float32(SURFACE_RADIUS) * surface_table()
    kern, scratch = make_kernel(bits, count)
    vmem = pl.BlockSpec(memory_space=pltpu.VMEM)
    return pl.pallas_call(
        kern,
        out_shape=jax.ShapeDtypeStruct((PROBES, LEAVES * PTS), f32),
        in_specs=[vmem] * 11,
        out_specs=vmem,
        scratch_shapes=scratch,
        name="fmm_apply",
        compiler_params=pltpu.CompilerParams(
            collective_id=0, has_side_effects=True, vmem_limit_bytes=60 << 20
        ),
    )(
        offsets, charges, counts.reshape(1, LEAVES), u_list, v_src, v_type,
        wanted.reshape(bits, CAP), m2l, uc2e, dc2e, jnp.asarray(surface),
    )


def solution(mesh):
    in_specs = (
        P(None, "cube"),
        P(None, "cube"),
        P("cube"),
        P("cube", None),
        P("cube", None),
        P("cube", None),
        P("cube", None, None),
        P(),
        P(),
        P(),
    )
    out_specs = P(None, "cube")
    return jax.shard_map(shards, mesh=mesh, in_specs=in_specs, out_specs=out_specs, check_vma=False)
```

```python
import math

import jax
import jax.numpy as jnp
import numpy as np
from jax import lax
from jax.experimental import pallas as pl
from jax.experimental.pallas import tpu as pltpu
from jax.sharding import PartitionSpec as P

GHOST = 8
SOFTEN = 0.01
INV_FOUR_PI = 1.0 / (4.0 * math.pi)
SURFACE_RADIUS = 0.55

LEAVES = 32
PTS = 128
PROBES = 16
EQUIV = 152
TYPES = 16
U_SLOTS = 27
V_SLOTS = 32
CAP = 16
EXT = LEAVES + 2 * GHOST
REACH = 2 * GHOST + 1
CHUNKS = 4
QC = PROBES // CHUNKS
REM = EQUIV - 128
CW = QC * 128 + QC * 32
KW = TYPES * 128 + TYPES * 32
MESH = pl.DeviceIdType.MESH
f32, bf16 = jnp.float32, jnp.bfloat16


def surface_table():
    lattice = np.arange(6)
    coords = np.stack(np.meshgrid(lattice, lattice, lattice, indexing="ij"), 0).reshape(3, -1)
    coords = (coords - 2.5) / 2.5
    on_face = np.max(np.abs(coords), axis=0) > 0.99
    return coords[:, on_face].astype(np.float32)


def dot_nt(a, b):
    return lax.dot_general(a, b, (((1,), (1,)), ((), ())), preferred_element_type=f32)


def dot_nn(a, b):
    return lax.dot_general(a, b, (((1,), (0,)), ((), ())), preferred_element_type=f32)


def split(x):
    high = x.astype(bf16)
    return high, (x - high.astype(f32)).astype(bf16)


def split3(x):
    first = x.astype(bf16).astype(f32)
    rest = x - first
    second = rest.astype(bf16).astype(f32)
    return first, second, rest - second


def iota(shape, dim):
    return lax.broadcasted_iota(jnp.int32, shape, dim)


def source_rows(x):
    row = iota(x.shape, 0)
    x = jnp.where(row < 3, x, 0.0)
    norm = jnp.sum(x * x, axis=0, keepdims=True) + SOFTEN
    e = jnp.where(row == 3, norm, jnp.where(row == 4, 1.0, x))
    a, b, c = split3(e)
    return jnp.concatenate([a, b, a, c, a, b], axis=0)


def target_rows(x):
    row = iota(x.shape, 0)
    x = jnp.where(row < 3, x, 0.0)
    norm = jnp.sum(x * x, axis=0, keepdims=True)
    e = jnp.where(row == 3, 1.0, jnp.where(row == 4, norm, -2.0 * x))
    a, b, c = split3(e)
    return jnp.concatenate([a, a, b, a, c, b], axis=0)


def column(row_vec, n, shift):
    m = row_vec.shape[1]
    wide = jnp.broadcast_to(row_vec.astype(f32), (n, m))
    hit = iota((n, m), 1) == iota((n, m), 0) + shift
    return jnp.sum(jnp.where(hit, wide, 0.0), axis=1, keepdims=True)


def lanes(i, width=128):
    return pl.ds(pl.multiple_of(i * width, width), width)


def make_kernel(bits, count):
    rows = bits * CAP + LEAVES

    def kern(off, chg, cnt, ulist, vsrc, vtype, wanted, m2l, uc, dc, surf, out,
             c3, pts, mq, cntb, mult, fs, dist_a, dist_b, kh_s, kl_s, chk, up, ups, stage, got, tlf, tl,
             mh, ml, turned, lm, near, dq, uch, ucl, dch, dcl, hoff, hchg, hcnt, wrecv,
             w_ss, w_rs, h_ss, h_rs, d_ss, d_rs):
        me = lax.axis_index("cube")
        first = me * LEAVES
        partners = [jnp.bitwise_xor(me, 1 << b) for b in range(bits)]
        nxt = lax.rem(me + 1, count)
        prv = lax.rem(me + count - 1, count)

        barrier = pltpu.get_barrier_semaphore()
        for other in partners + [nxt, prv]:
            pl.semaphore_signal(barrier, inc=1, device_id=(other,), device_id_type=MESH)

        ids = first - GHOST + iota((8, 128), 1)
        axis = iota((8, 128), 0)
        corner = jnp.zeros((8, 128), jnp.int32)
        for digit in range(5):
            corner = corner + ((lax.shift_right_arithmetic(ids, axis + 3 * digit) & 1) << digit)
        corner = jnp.where(axis < 3, corner, 0).astype(f32)
        for h in range(EXT):
            c3[h] = jnp.broadcast_to(corner[:, h:h + 1], (8, 128))
        lane = iota((PROBES, PTS), 1).astype(f32)
        pts[...] = jnp.zeros((EXT, 8, 128), f32)
        cntb[GHOST:GHOST + LEAVES, :] = jnp.broadcast_to(column(cnt[...], LEAVES, 0), (LEAVES, 128))

        def place(h, position, charge):
            pts[h, 0:3, :] = position + c3[h, 0:3, :]
            live = lane < cntb[pl.ds(h, 1), :]
            mq[h] = jnp.where(live, charge, 0.0) * INV_FOUR_PI

        def own_leaf(l, carry):
            place(l + GHOST, off[:, lanes(l)], chg[:, lanes(l)])
            return carry

        lax.fori_loop(0, LEAVES, own_leaf, 0, unroll=4)

        uch[...] = jnp.zeros(uch.shape, bf16)
        ucl[...] = jnp.zeros(ucl.shape, bf16)
        u_h, u_l = split(uc[...])
        uch[0:128, 0:EQUIV] = u_h[0:128]
        ucl[0:128, 0:EQUIV] = u_l[0:128]
        for g in range(4):
            uch[128 + 32 * g:128 + 32 * g + REM, 0:EQUIV] = u_h[128:EQUIV]
            ucl[128 + 32 * g:128 + 32 * g + REM, 0:EQUIV] = u_l[128:EQUIV]
        chk[1] = jnp.zeros((PROBES * LEAVES, 128), f32)
        surf_cols = jnp.transpose(source_rows(surf[...]))[:EQUIV].astype(bf16)

        def upward(i, carry):
            sides = []
            for k in range(2):
                h = 2 * i + k + GHOST
                sides.append(target_rows(pts[h] - (c3[h] + 0.5)).astype(bf16))
            tile = lax.rsqrt(dot_nn(surf_cols, jnp.concatenate(sides, 1)))
            k_h, k_l = split(tile)
            kh_s[i] = k_h
            kl_s[i] = k_l
            for k in range(2):
                l = 2 * i + k
                part = slice(k * 128, (k + 1) * 128)
                q_h, q_l = split(mq[l + GHOST])
                both = dot_nt(jnp.concatenate([q_h, q_l], 0), k_h[:, part])
                check = both[:PROBES] + both[PROBES:] + dot_nt(q_h, k_l[:, part])
                chk[0, pl.ds(l, PROBES, stride=LEAVES), :] = check[:, :128]
                chk[1, pl.ds(l, PROBES, stride=LEAVES), 0:REM] = check[:, 128:]
            return carry

        lax.fori_loop(0, LEAVES // 2, upward, 0, unroll=2)
        c_h, c_l = split(jnp.concatenate([chk[0], chk[1]], 1))
        dens = dot_nt(c_h, uch[...]) + dot_nt(c_l, uch[...]) + dot_nt(c_h, ucl[...])
        group_of = iota((LEAVES, 128), 1) // 32
        for q in range(PROBES):
            c, qq = q // QC, q % QC
            up[c, :, qq * 128:(qq + 1) * 128] = dens[q * LEAVES:(q + 1) * LEAVES, :128]
        for k in range(PROBES // 4):
            c, kk = (4 * k) // QC, k % (QC // 4)
            total = jnp.zeros((LEAVES, 128), f32)
            for g in range(4):
                q = 4 * k + g
                total = jnp.where(group_of == g, dens[q * LEAVES:(q + 1) * LEAVES, 128:], total)
            up[c, :, QC * 128 + kk * 128:QC * 128 + (kk + 1) * 128] = total
        for c in range(CHUNKS):
            value = up[c]
            got[c, bits * CAP:rows, :] = value
            a, b, d = split3(value)
            ups[c] = jnp.concatenate([a, b, d], 0).astype(bf16)

        pl.semaphore_wait(barrier, bits + 2)
        def want(b):
            return pltpu.make_async_remote_copy(
                src_ref=wanted, dst_ref=wrecv.at[b], send_sem=w_ss.at[b], recv_sem=w_rs.at[b],
                device_id=(partners[b],), device_id_type=MESH)

        for b in range(bits):
            want(b).start()
        halos = []
        width = GHOST * PTS
        for side, other, begin in ((0, nxt, LEAVES * PTS - width), (1, prv, 0)):
            for k, (src, dst) in enumerate((
                    (off.at[:, pl.ds(begin, width)], hoff.at[side]),
                    (chg.at[:, pl.ds(begin, width)], hchg.at[side]),
                    (cnt, hcnt.at[side]))):
                halos.append(pltpu.make_async_remote_copy(
                    src_ref=src, dst_ref=dst, send_sem=h_ss.at[side, k], recv_sem=h_rs.at[side, k],
                    device_id=(other,), device_id_type=MESH))
                halos[-1].start()

        rel = ulist[...] - (first - GHOST) - iota((LEAVES, U_SLOTS), 0)
        for o in range(REACH):
            hits = jnp.sum(jnp.where(rel == o, 1.0, 0.0), axis=1, keepdims=True)
            mult[o] = jnp.broadcast_to(hits, (LEAVES, 128))

        def tally(l, carry):
            kinds = jnp.broadcast_to(vtype[pl.ds(l, 1), :], (TYPES, V_SLOTS))
            codes = jnp.broadcast_to(vsrc[pl.ds(l, 1), :], (256, V_SLOTS))
            of_kind = jnp.where(kinds == iota((TYPES, V_SLOTS), 0), 1.0, 0.0).astype(bf16)
            of_code = jnp.where(codes == iota((256, V_SLOTS), 0), 1.0, 0.0).astype(bf16)
            found = dot_nt(of_kind, of_code)
            tlf[0, pl.ds(l, TYPES, stride=LEAVES), :] = found[:, :128]
            tlf[1, pl.ds(l, TYPES, stride=LEAVES), :] = found[:, 128:]
            return carry

        lax.fori_loop(0, LEAVES, tally, 0, unroll=4)
        tl[...] = jnp.concatenate([tlf[0], tlf[1]], 1)[:, :rows].astype(bf16)

        for n in range(TYPES * EQUIV // 128):
            turned[n * 128:(n + 1) * 128, :] = jnp.transpose(m2l[:, n * 128:(n + 1) * 128])
        for t in range(TYPES):
            a, b = split(turned[t * EQUIV:t * EQUIV + 128, :])
            mh[t * 128:(t + 1) * 128, :] = a
            ml[t * 128:(t + 1) * 128, :] = b
            a, b = split(jnp.concatenate(
                [turned[t * EQUIV + 128:(t + 1) * EQUIV, :], jnp.zeros((32 - REM, EQUIV), f32)], 0))
            mh[TYPES * 128 + t * 32:TYPES * 128 + (t + 1) * 32, :] = a
            ml[TYPES * 128 + t * 32:TYPES * 128 + (t + 1) * 32, :] = b
        d_h, d_l = split(dc[...] * INV_FOUR_PI)
        dch[...] = d_h
        dcl[...] = d_l

        def send(c, b):
            return pltpu.make_async_remote_copy(
                src_ref=stage.at[c, pl.ds(b * CAP, CAP)], dst_ref=got.at[c, pl.ds(b * CAP, CAP)],
                send_sem=d_ss.at[c, b], recv_sem=d_rs.at[c, b],
                device_id=(partners[b],), device_id_type=MESH)

        def serve(chosen):
            picks = []
            for b in chosen:
                want(b).wait()
                listed = column(wrecv[b, b:b + 1, :], CAP, 0)
                slot = (iota((CAP, 3 * LEAVES), 1) % LEAVES).astype(f32)
                picks.append(jnp.where(listed == slot, 1.0, 0.0))
            pick = jnp.concatenate(picks, 0).astype(bf16)
            for c in range(CHUNKS):
                taken = dot_nn(pick, ups[c])
                for k, b in enumerate(chosen):
                    stage[c, b * CAP:(b + 1) * CAP, :] = taken[k * CAP:(k + 1) * CAP]
                for b in chosen:
                    send(c, b).start()

        far_bits = [b for b in (4,) if b < bits]
        near_bits = [b for b in (3, 2, 1, 6, 8, 5, 7, 0) if b < bits]
        order = far_bits + near_bits
        serve(near_bits)

        def block_of(l):
            return l // 8, c3[(l // 8) * 8 + GHOST] + 1.0

        def distances(l, slot, dest):
            base, middle = block_of(l)
            rows_t = jnp.transpose(target_rows(pts[l + GHOST] - middle)).astype(bf16)
            at = l - base * 8
            for o in range(0, REACH, 2):
                both = [o, o + 1] if o + 1 < REACH else [o]
                src = jnp.concatenate([fs[slot, at + k] for k in both], 1)
                dest[:, o * 128:(o + len(both)) * 128] = dot_nn(rows_t, src)

        def reduce(l, dist):
            acc = jnp.zeros((2 * PROBES, PTS), f32)
            acc_l = jnp.zeros((PROBES, PTS), f32)
            for o in range(0, REACH, 2):
                both = [o, o + 1] if o + 1 < REACH else [o]
                k_h, k_l = split(lax.rsqrt(dist[:, o * 128:(o + len(both)) * 128]))
                weighted = jnp.concatenate([mq[l + k] * mult[k, pl.ds(l, 1), :] for k in both], 1)
                w_h, w_l = split(weighted)
                acc = acc + dot_nt(jnp.concatenate([w_h, w_l], 0), k_h)
                acc_l = acc_l + dot_nt(w_h, k_l)
            near[:, lanes(l)] = acc[:PROBES] + acc[PROBES:] + acc_l

        def near_half(half, carry):
            @pl.when(half == 1)
            def _():
                for copy in halos:
                    copy.wait()
                cntb[0:GHOST, :] = jnp.broadcast_to(column(hcnt[0], GHOST, LEAVES - GHOST), (GHOST, 128))
                cntb[LEAVES + GHOST:EXT, :] = jnp.broadcast_to(column(hcnt[1], GHOST, 0), (GHOST, 128))
                for side, h0 in ((0, 0), (1, LEAVES + GHOST)):
                    for k in range(GHOST):
                        place(h0 + k, hoff[side, :, k * PTS:(k + 1) * PTS],
                              hchg[side, :, k * PTS:(k + 1) * PTS])

            def leaf(i):
                return lax.rem(GHOST + half * 16 + i, LEAVES)

            def prepare(k, inner):
                for slot in range(2):
                    base = (leaf(8 * slot) // 8) * 8
                    fs[slot, k] = source_rows(pts[base + k] - (c3[base + GHOST] + 1.0)).astype(bf16)
                return inner

            lax.fori_loop(0, 8 + 2 * GHOST, prepare, 0, unroll=2)
            distances(leaf(0), 0, dist_a)

            def pair(j, inner):
                if far_bits:
                    @pl.when((half == 0) & (j == 2))
                    def _():
                        serve(far_bits)
                l0, l1 = leaf(2 * j), leaf(2 * j + 1)
                i2 = jnp.minimum(2 * j + 2, 15)
                distances(l1, j // 4, dist_b)
                reduce(l0, dist_a)
                distances(leaf(i2), i2 // 8, dist_a)
                reduce(l1, dist_b)
                return inner

            lax.fori_loop(0, 8, pair, 0)
            return carry

        lax.fori_loop(0, 2, near_half, 0)

        lane_g = iota((LEAVES, 128), 1) // 32
        for c in range(CHUNKS):
            for b in order:
                send(c, b).wait()
            tallied = tl[...]
            for n in range(QC // 2):
                g_h, g_l = split(got[c, :, n * 256:(n + 1) * 256])
                b_h, b_l = split(dot_nn(tallied, g_h) + dot_nn(tallied, g_l))
                for t in range(TYPES):
                    for k in range(2):
                        qq = 2 * n + k
                        r = slice(qq * LEAVES, (qq + 1) * LEAVES)
                        r2 = slice((QC + qq) * LEAVES, (QC + qq + 1) * LEAVES)
                        s = slice(t * 128, (t + 1) * 128)
                        lm[r, s] = b_h[t * LEAVES:(t + 1) * LEAVES, k * 128:(k + 1) * 128]
                        lm[r2, s] = b_l[t * LEAVES:(t + 1) * LEAVES, k * 128:(k + 1) * 128]
            g_h, g_l = split(got[c, :, QC * 128:])
            by = dot_nn(tallied, g_h) + dot_nn(tallied, g_l)
            for g in range(QC):
                for tt in range(TYPES // 4):
                    total = jnp.zeros((LEAVES, 128), f32)
                    for j in range(4):
                        t = 4 * tt + j
                        part = by[t * LEAVES:(t + 1) * LEAVES]
                        turn = (32 * (j - g)) % 128
                        if turn:
                            part = pltpu.roll(part, turn, 1)
                        total = jnp.where(lane_g == j, part, total)
                    b_h, b_l = split(total)
                    r = slice(g * LEAVES, (g + 1) * LEAVES)
                    r2 = slice((QC + g) * LEAVES, (QC + g + 1) * LEAVES)
                    s = slice(TYPES * 128 + tt * 128, TYPES * 128 + (tt + 1) * 128)
                    lm[r, s] = b_h
                    lm[r2, s] = b_l
            half = QC * LEAVES
            with_h = dot_nn(lm[...], mh[...])
            down = with_h[:half] + with_h[half:] + dot_nn(lm[0:half], ml[...])
            w_h, w_l = split(down)
            eq = dot_nt(w_h, dch[...]) + dot_nt(w_l, dch[...]) + dot_nt(w_h, dcl[...])
            dq[c, 0] = eq[:, :128]
            dq[c, 1, :, 0:REM] = eq[:, 128:]
            if c < CHUNKS - 2:
                continue
            ready = [c] if c == CHUNKS - 1 else list(range(c + 1))
            probes = slice(ready[0] * QC, (ready[-1] + 1) * QC)
            many = len(ready) * QC

            def far(i, carry):
                for k in range(2):
                    l = 2 * i + k
                    e = jnp.concatenate([
                        jnp.concatenate([dq[m, 0, pl.ds(l, QC, stride=LEAVES), :],
                                         dq[m, 1, pl.ds(l, QC, stride=LEAVES), 0:REM]], 1)
                        for m in ready], 0)
                    high = e.astype(bf16).astype(f32)
                    both = jnp.concatenate([high, e - high], 0).astype(bf16)
                    cols = slice(k * 128, (k + 1) * 128)
                    part = dot_nn(both, kh_s[i, :, cols])
                    part_l = dot_nn(both, kl_s[i, :, cols])
                    value = part[:many] + part[many:] + part_l[:many]
                    live = iota((many, PTS), 1).astype(f32) < cntb[pl.ds(l + GHOST, 1), :]
                    out[probes, lanes(l)] = jnp.where(live, near[probes, lanes(l)] + value, 0.0)
                return carry

            lax.fori_loop(0, LEAVES // 2, far, 0, unroll=2)

    scratch = [
        pltpu.VMEM((EXT, 8, 128), f32),
        pltpu.VMEM((EXT, 8, 128), f32),
        pltpu.VMEM((EXT, PROBES, PTS), f32),
        pltpu.VMEM((EXT, 128), f32),
        pltpu.VMEM((REACH, LEAVES, 128), f32),
        pltpu.VMEM((2, 8 + 2 * GHOST, 48, 128), bf16),
        pltpu.VMEM((PTS, REACH * 128), f32),
        pltpu.VMEM((PTS, REACH * 128), f32),
        pltpu.VMEM((LEAVES // 2, EQUIV, 256), bf16),
        pltpu.VMEM((LEAVES // 2, EQUIV, 256), bf16),
        pltpu.VMEM((2, PROBES * LEAVES, 128), f32),
        pltpu.VMEM((CHUNKS, LEAVES, CW), f32),
        pltpu.VMEM((CHUNKS, 3 * LEAVES, CW), bf16),
        pltpu.VMEM((CHUNKS, bits * CAP, CW), f32),
        pltpu.VMEM((CHUNKS, rows, CW), f32),
        pltpu.VMEM((2, TYPES * LEAVES, 128), f32),
        pltpu.VMEM((TYPES * LEAVES, rows), bf16),
        pltpu.VMEM((KW, EQUIV), bf16),
        pltpu.VMEM((KW, EQUIV), bf16),
        pltpu.VMEM((TYPES * EQUIV, EQUIV), f32),
        pltpu.VMEM((2 * QC * LEAVES, KW), bf16),
        pltpu.VMEM((PROBES, LEAVES * PTS), f32),
        pltpu.VMEM((CHUNKS, 2, QC * LEAVES, 128), f32),
        pltpu.VMEM((256, 256), bf16),
        pltpu.VMEM((256, 256), bf16),
        pltpu.VMEM((EQUIV, EQUIV), bf16),
        pltpu.VMEM((EQUIV, EQUIV), bf16),
        pltpu.VMEM((2, 3, GHOST * PTS), f32),
        pltpu.VMEM((2, PROBES, GHOST * PTS), f32),
        pltpu.VMEM((2, 1, LEAVES), jnp.int32),
        pltpu.VMEM((bits, bits, CAP), jnp.int32),
        pltpu.SemaphoreType.DMA((bits,)),
        pltpu.SemaphoreType.DMA((bits,)),
        pltpu.SemaphoreType.DMA((2, 3)),
        pltpu.SemaphoreType.DMA((2, 3)),
        pltpu.SemaphoreType.DMA((CHUNKS, bits)),
        pltpu.SemaphoreType.DMA((CHUNKS, bits)),
    ]
    return kern, scratch


def shards(offsets, charges, counts, u_list, v_src, v_type, wanted, m2l, uc2e, dc2e):
    count = lax.axis_size("cube")
    bits = count.bit_length() - 1
    surface = np.zeros((8, 256), np.float32)
    surface[:3, :EQUIV] = np.float32(SURFACE_RADIUS) * surface_table()
    kern, scratch = make_kernel(bits, count)
    vmem = pl.BlockSpec(memory_space=pltpu.VMEM)
    return pl.pallas_call(
        kern,
        out_shape=jax.ShapeDtypeStruct((PROBES, LEAVES * PTS), f32),
        in_specs=[vmem] * 11,
        out_specs=vmem,
        scratch_shapes=scratch,
        name="fmm_apply",
        compiler_params=pltpu.CompilerParams(
            collective_id=0, has_side_effects=True, vmem_limit_bytes=60 << 20
        ),
    )(
        offsets, charges, counts.reshape(1, LEAVES), u_list, v_src, v_type,
        wanted.reshape(bits, CAP), m2l, uc2e, dc2e, jnp.asarray(surface),
    )


def solution(mesh):
    in_specs = (
        P(None, "cube"),
        P(None, "cube"),
        P("cube"),
        P("cube", None),
        P("cube", None),
        P("cube", None),
        P("cube", None, None),
        P(),
        P(),
        P(),
    )
    out_specs = P(None, "cube")
    return jax.shard_map(shards, mesh=mesh, in_specs=in_specs, out_specs=out_specs, check_vma=False)
```

```python
import math

import jax
import jax.numpy as jnp
import numpy as np
from jax import lax
from jax.experimental import pallas as pl
from jax.experimental.pallas import tpu as pltpu
from jax.sharding import PartitionSpec as P

GHOST = 8
SOFTEN = 0.01
INV_FOUR_PI = 1.0 / (4.0 * math.pi)
SURFACE_RADIUS = 0.55

LEAVES = 32
PTS = 128
PROBES = 16
EQUIV = 152
TYPES = 16
U_SLOTS = 27
V_SLOTS = 32
CAP = 16
EXT = LEAVES + 2 * GHOST
REACH = 2 * GHOST + 1
CHUNKS = 4
QC = PROBES // CHUNKS
STARTS = (2, 6, 10)
REM = EQUIV - 128
CW = QC * 128 + QC * 32
KW = TYPES * 128 + TYPES * 32
MESH = pl.DeviceIdType.MESH
f32, bf16 = jnp.float32, jnp.bfloat16


def surface_table():
    lattice = np.arange(6)
    coords = np.stack(np.meshgrid(lattice, lattice, lattice, indexing="ij"), 0).reshape(3, -1)
    coords = (coords - 2.5) / 2.5
    on_face = np.max(np.abs(coords), axis=0) > 0.99
    return coords[:, on_face].astype(np.float32)


def dot_nt(a, b):
    return lax.dot_general(a, b, (((1,), (1,)), ((), ())), preferred_element_type=f32)


def dot_nn(a, b):
    return lax.dot_general(a, b, (((1,), (0,)), ((), ())), preferred_element_type=f32)


def split(x):
    high = x.astype(bf16)
    return high, (x - high.astype(f32)).astype(bf16)


def split3(x):
    first = x.astype(bf16).astype(f32)
    rest = x - first
    second = rest.astype(bf16).astype(f32)
    return first, second, rest - second


def iota(shape, dim):
    return lax.broadcasted_iota(jnp.int32, shape, dim)


def source_rows(x):
    row = iota(x.shape, 0)
    x = jnp.where(row < 3, x, 0.0)
    norm = jnp.sum(x * x, axis=0, keepdims=True) + SOFTEN
    e = jnp.where(row == 3, norm, jnp.where(row == 4, 1.0, x))
    a, b, c = split3(e)
    return jnp.concatenate([a, b, a, c, a, b], axis=0)


def target_rows(x):
    row = iota(x.shape, 0)
    x = jnp.where(row < 3, x, 0.0)
    norm = jnp.sum(x * x, axis=0, keepdims=True)
    e = jnp.where(row == 3, 1.0, jnp.where(row == 4, norm, -2.0 * x))
    a, b, c = split3(e)
    return jnp.concatenate([a, a, b, a, c, b], axis=0)


def column(row_vec, n, shift):
    m = row_vec.shape[1]
    wide = jnp.broadcast_to(row_vec.astype(f32), (n, m))
    hit = iota((n, m), 1) == iota((n, m), 0) + shift
    return jnp.sum(jnp.where(hit, wide, 0.0), axis=1, keepdims=True)


def lanes(i, width=128):
    return pl.ds(pl.multiple_of(i * width, width), width)


def make_kernel(bits, count):
    rows = bits * CAP + LEAVES

    def kern(off, chg, cnt, ulist, vsrc, vtype, wanted, m2l, uc, dc, surf, out,
             c3, pts, mq, cntb, mult, fs, dist_a, dist_b, kh_s, kl_s, chk, up, ups, stage, got, tlf, tl,
             mh, ml, turned, lm, halves, near, dq, uch, ucl, dch, dcl, hoff, hchg, hcnt, wrecv,
             w_ss, w_rs, h_ss, h_rs, d_ss, d_rs):
        me = lax.axis_index("cube")
        first = me * LEAVES
        partners = [jnp.bitwise_xor(me, 1 << b) for b in range(bits)]
        nxt = lax.rem(me + 1, count)
        prv = lax.rem(me + count - 1, count)

        barrier = pltpu.get_barrier_semaphore()
        for other in partners + [nxt, prv]:
            pl.semaphore_signal(barrier, inc=1, device_id=(other,), device_id_type=MESH)

        ids = first - GHOST + iota((8, 128), 1)
        axis = iota((8, 128), 0)
        corner = jnp.zeros((8, 128), jnp.int32)
        for digit in range(5):
            corner = corner + ((lax.shift_right_arithmetic(ids, axis + 3 * digit) & 1) << digit)
        corner = jnp.where(axis < 3, corner, 0).astype(f32)
        for h in range(EXT):
            c3[h] = jnp.broadcast_to(corner[:, h:h + 1], (8, 128))
        lane = iota((PROBES, PTS), 1).astype(f32)
        pts[...] = jnp.zeros((EXT, 8, 128), f32)
        cntb[GHOST:GHOST + LEAVES, :] = jnp.broadcast_to(column(cnt[...], LEAVES, 0), (LEAVES, 128))

        def place(h, position, charge):
            pts[h, 0:3, :] = position + c3[h, 0:3, :]
            live = lane < cntb[pl.ds(h, 1), :]
            mq[h] = jnp.where(live, charge, 0.0) * INV_FOUR_PI

        def own_leaf(l, carry):
            place(l + GHOST, off[:, lanes(l)], chg[:, lanes(l)])
            return carry

        lax.fori_loop(0, LEAVES, own_leaf, 0, unroll=4)

        def want(b):
            return pltpu.make_async_remote_copy(
                src_ref=wanted, dst_ref=wrecv.at[b], send_sem=w_ss.at[b], recv_sem=w_rs.at[b],
                device_id=(partners[b],), device_id_type=MESH)

        def halo_copies():
            halos = []
            width = GHOST * PTS
            for side, other, begin in ((0, nxt, LEAVES * PTS - width), (1, prv, 0)):
                for k, (src, dst) in enumerate((
                        (off.at[:, pl.ds(begin, width)], hoff.at[side]),
                        (chg.at[:, pl.ds(begin, width)], hchg.at[side]),
                        (cnt, hcnt.at[side]))):
                    halos.append(pltpu.make_async_remote_copy(
                        src_ref=src, dst_ref=dst, send_sem=h_ss.at[side, k], recv_sem=h_rs.at[side, k],
                        device_id=(other,), device_id_type=MESH))
            return halos

        def greet():
            pl.semaphore_wait(barrier, bits + 2)
            for b in range(bits):
                want(b).start()
            for copy in halo_copies():
                copy.start()

        uch[...] = jnp.zeros(uch.shape, bf16)
        ucl[...] = jnp.zeros(ucl.shape, bf16)
        u_h, u_l = split(uc[...])
        uch[0:128, 0:EQUIV] = u_h[0:128]
        ucl[0:128, 0:EQUIV] = u_l[0:128]
        for g in range(4):
            uch[128 + 32 * g:128 + 32 * g + REM, 0:EQUIV] = u_h[128:EQUIV]
            ucl[128 + 32 * g:128 + 32 * g + REM, 0:EQUIV] = u_l[128:EQUIV]
        chk[1] = jnp.zeros((PROBES * LEAVES, 128), f32)
        surf_cols = jnp.transpose(source_rows(surf[...]))[:EQUIV].astype(bf16)

        def upward(j, carry):
            upward_pair(2 * j)
            upward_pair(2 * j + 1)

            @pl.when(j == 5)
            def _():
                greet()

            return carry

        def upward_pair(i):
            sides = []
            for k in range(2):
                h = 2 * i + k + GHOST
                sides.append(target_rows(pts[h] - (c3[h] + 0.5)).astype(bf16))
            tile = lax.rsqrt(dot_nn(surf_cols, jnp.concatenate(sides, 1)))
            k_h, k_l = split(tile)
            kh_s[i] = k_h
            kl_s[i] = k_l
            for k in range(2):
                l = 2 * i + k
                part = slice(k * 128, (k + 1) * 128)
                q_h, q_l = split(mq[l + GHOST])
                both = dot_nt(jnp.concatenate([q_h, q_l], 0), k_h[:, part])
                check = both[:PROBES] + both[PROBES:] + dot_nt(q_h, k_l[:, part])
                chk[0, pl.ds(l, PROBES, stride=LEAVES), :] = check[:, :128]
                chk[1, pl.ds(l, PROBES, stride=LEAVES), 0:REM] = check[:, 128:]

        lax.fori_loop(0, LEAVES // 4, upward, 0)
        c_h, c_l = split(jnp.concatenate([chk[0], chk[1]], 1))
        dens = dot_nt(c_h, uch[...]) + dot_nt(c_l, uch[...]) + dot_nt(c_h, ucl[...])
        group_of = iota((LEAVES, 128), 1) // 32
        for q in range(PROBES):
            c, qq = q // QC, q % QC
            up[c, :, qq * 128:(qq + 1) * 128] = dens[q * LEAVES:(q + 1) * LEAVES, :128]
        for k in range(PROBES // 4):
            c, kk = (4 * k) // QC, k % (QC // 4)
            total = jnp.zeros((LEAVES, 128), f32)
            for g in range(4):
                q = 4 * k + g
                total = jnp.where(group_of == g, dens[q * LEAVES:(q + 1) * LEAVES, 128:], total)
            up[c, :, QC * 128 + kk * 128:QC * 128 + (kk + 1) * 128] = total
        for c in range(CHUNKS):
            value = up[c]
            got[c, bits * CAP:rows, :] = value
            a, b, d = split3(value)
            ups[c] = jnp.concatenate([a, b, d], 0).astype(bf16)

        rel = ulist[...] - (first - GHOST) - iota((LEAVES, U_SLOTS), 0)
        for o in range(REACH):
            hits = jnp.sum(jnp.where(rel == o, 1.0, 0.0), axis=1, keepdims=True)
            mult[o] = jnp.broadcast_to(hits, (LEAVES, 128))

        def tally(l, carry):
            kinds = jnp.broadcast_to(vtype[pl.ds(l, 1), :], (TYPES, V_SLOTS))
            codes = jnp.broadcast_to(vsrc[pl.ds(l, 1), :], (256, V_SLOTS))
            of_kind = jnp.where(kinds == iota((TYPES, V_SLOTS), 0), 1.0, 0.0).astype(bf16)
            of_code = jnp.where(codes == iota((256, V_SLOTS), 0), 1.0, 0.0).astype(bf16)
            found = dot_nt(of_kind, of_code)
            tlf[0, pl.ds(l, TYPES, stride=LEAVES), :] = found[:, :128]
            tlf[1, pl.ds(l, TYPES, stride=LEAVES), :] = found[:, 128:]
            return carry

        lax.fori_loop(0, LEAVES, tally, 0, unroll=4)
        tl[...] = jnp.concatenate([tlf[0], tlf[1]], 1)[:, :rows].astype(bf16)

        def send(c, b):
            return pltpu.make_async_remote_copy(
                src_ref=stage.at[c, pl.ds(b * CAP, CAP)], dst_ref=got.at[c, pl.ds(b * CAP, CAP)],
                send_sem=d_ss.at[c, b], recv_sem=d_rs.at[c, b],
                device_id=(partners[b],), device_id_type=MESH)

        def serve(chosen):
            picks = []
            for b in chosen:
                want(b).wait()
                listed = column(wrecv[b, b:b + 1, :], CAP, 0)
                slot = (iota((CAP, 3 * LEAVES), 1) % LEAVES).astype(f32)
                picks.append(jnp.where(listed == slot, 1.0, 0.0))
            pick = jnp.concatenate(picks, 0).astype(bf16)
            for c in range(CHUNKS):
                taken = dot_nn(pick, ups[c])
                for k, b in enumerate(chosen):
                    stage[c, b * CAP:(b + 1) * CAP, :] = taken[k * CAP:(k + 1) * CAP]
            for b in chosen:
                send(0, b).start()

        far_bits = [b for b in (4,) if b < bits]
        near_bits = [b for b in (3, 2, 1, 6, 8, 5, 7, 0) if b < bits]
        order = far_bits + near_bits
        serve(near_bits)

        for n in range(TYPES * EQUIV // 128):
            turned[n * 128:(n + 1) * 128, :] = jnp.transpose(m2l[:, n * 128:(n + 1) * 128])
        for t in range(TYPES):
            a, b = split(turned[t * EQUIV:t * EQUIV + 128, :])
            mh[t * 128:(t + 1) * 128, :] = a
            ml[t * 128:(t + 1) * 128, :] = b
            a, b = split(jnp.concatenate(
                [turned[t * EQUIV + 128:(t + 1) * EQUIV, :], jnp.zeros((32 - REM, EQUIV), f32)], 0))
            mh[TYPES * 128 + t * 32:TYPES * 128 + (t + 1) * 32, :] = a
            ml[TYPES * 128 + t * 32:TYPES * 128 + (t + 1) * 32, :] = b
        d_h, d_l = split(dc[...] * INV_FOUR_PI)
        dch[...] = d_h
        dcl[...] = d_l
        serve(far_bits)

        def block_of(l):
            return l // 8, c3[(l // 8) * 8 + GHOST] + 1.0

        def distances(l, slot, dest):
            base, middle = block_of(l)
            rows_t = jnp.transpose(target_rows(pts[l + GHOST] - middle)).astype(bf16)
            at = l - base * 8
            for o in range(0, REACH, 2):
                both = [o, o + 1] if o + 1 < REACH else [o]
                src = jnp.concatenate([fs[slot, at + k] for k in both], 1)
                dest[:, o * 128:(o + len(both)) * 128] = dot_nn(rows_t, src)

        def reduce(l, dist):
            acc = jnp.zeros((2 * PROBES, PTS), f32)
            acc_l = jnp.zeros((PROBES, PTS), f32)
            for o in range(0, REACH, 2):
                both = [o, o + 1] if o + 1 < REACH else [o]
                k_h, k_l = split(lax.rsqrt(dist[:, o * 128:(o + len(both)) * 128]))
                weighted = jnp.concatenate([mq[l + k] * mult[k, pl.ds(l, 1), :] for k in both], 1)
                w_h, w_l = split(weighted)
                acc = acc + dot_nt(jnp.concatenate([w_h, w_l], 0), k_h)
                acc_l = acc_l + dot_nt(w_h, k_l)
            near[:, lanes(l)] = acc[:PROBES] + acc[PROBES:] + acc_l

        def near_half(half, carry):
            @pl.when(half == 1)
            def _():
                for copy in halo_copies():
                    copy.wait()
                cntb[0:GHOST, :] = jnp.broadcast_to(column(hcnt[0], GHOST, LEAVES - GHOST), (GHOST, 128))
                cntb[LEAVES + GHOST:EXT, :] = jnp.broadcast_to(column(hcnt[1], GHOST, 0), (GHOST, 128))
                for side, h0 in ((0, 0), (1, LEAVES + GHOST)):
                    for k in range(GHOST):
                        place(h0 + k, hoff[side, :, k * PTS:(k + 1) * PTS],
                              hchg[side, :, k * PTS:(k + 1) * PTS])

            def leaf(i):
                return lax.rem(GHOST + half * 16 + i, LEAVES)

            def prepare(k, inner):
                for slot in range(2):
                    base = (leaf(8 * slot) // 8) * 8
                    fs[slot, k] = source_rows(pts[base + k] - (c3[base + GHOST] + 1.0)).astype(bf16)
                return inner

            lax.fori_loop(0, 8 + 2 * GHOST, prepare, 0, unroll=2)
            distances(leaf(0), 0, dist_a)

            def pair(j, inner):
                for c, when in enumerate(STARTS, 1):
                    @pl.when(half * 8 + j == when)
                    def _(c=c):
                        for b in order:
                            send(c, b).start()
                l0, l1 = leaf(2 * j), leaf(2 * j + 1)
                i2 = jnp.minimum(2 * j + 2, 15)
                distances(l1, j // 4, dist_b)
                reduce(l0, dist_a)
                distances(leaf(i2), i2 // 8, dist_a)
                reduce(l1, dist_b)
                return inner

            lax.fori_loop(0, 8, pair, 0)
            return carry

        lax.fori_loop(0, 2, near_half, 0)

        lane_g = iota((LEAVES, 128), 1) // 32
        for c in range(CHUNKS):
            for b in order:
                send(c, b).wait()
            for n in range(QC // 2):
                g_h, g_l = split(got[c, :, n * 256:(n + 1) * 256])
                upper = split(dot_nn(tl[:256], g_h) + dot_nn(tl[:256], g_l))
                lower = split(dot_nn(tl[256:], g_h) + dot_nn(tl[256:], g_l))
                for t in range(TYPES):
                    b_h, b_l = (x[(t % 8) * LEAVES:(t % 8 + 1) * LEAVES] for x in (upper, lower)[t // 8])
                    for k in range(2):
                        qq = 2 * n + k
                        r = slice(qq * LEAVES, (qq + 1) * LEAVES)
                        r2 = slice((QC + qq) * LEAVES, (QC + qq + 1) * LEAVES)
                        s = slice(t * 128, (t + 1) * 128)
                        lm[r, s] = b_h[:, k * 128:(k + 1) * 128]
                        lm[r2, s] = b_l[:, k * 128:(k + 1) * 128]
            g_h, g_l = split(got[c, :, QC * 128:])
            by = (dot_nn(tl[:256], g_h) + dot_nn(tl[:256], g_l), dot_nn(tl[256:], g_h) + dot_nn(tl[256:], g_l))
            for g in range(QC):
                for tt in range(TYPES // 4):
                    total = jnp.zeros((LEAVES, 128), f32)
                    for j in range(4):
                        t = 4 * tt + j
                        part = by[t // 8][(t % 8) * LEAVES:(t % 8 + 1) * LEAVES]
                        turn = (32 * (j - g)) % 128
                        if turn:
                            part = pltpu.roll(part, turn, 1)
                        total = jnp.where(lane_g == j, part, total)
                    b_h, b_l = split(total)
                    r = slice(g * LEAVES, (g + 1) * LEAVES)
                    r2 = slice((QC + g) * LEAVES, (QC + g + 1) * LEAVES)
                    s = slice(TYPES * 128 + tt * 128, TYPES * 128 + (tt + 1) * 128)
                    lm[r, s] = b_h
                    lm[r2, s] = b_l
            half = QC * LEAVES
            cut = KW // 2
            halves[0, :] = dot_nn(lm[:, :cut], mh[:cut])
            halves[1, :] = dot_nn(lm[:, cut:], mh[cut:])
            halves[0, :half] = halves[0, :half] + dot_nn(lm[0:half, :cut], ml[:cut])
            halves[1, :half] = halves[1, :half] + dot_nn(lm[0:half, cut:], ml[cut:])
            down = (halves[0, :half] + halves[0, half:]) + (halves[1, :half] + halves[1, half:])
            w_h, w_l = split(down)
            eq = dot_nt(w_h, dch[...]) + dot_nt(w_l, dch[...]) + dot_nt(w_h, dcl[...])
            dq[c, 0] = eq[:, :128]
            dq[c, 1, :, 0:REM] = eq[:, 128:]
            if c < CHUNKS - 2:
                continue
            ready = [c] if c == CHUNKS - 1 else list(range(c + 1))
            probes = slice(ready[0] * QC, (ready[-1] + 1) * QC)
            many = len(ready) * QC

            def far(i, carry):
                for k in range(2):
                    l = 2 * i + k
                    e = jnp.concatenate([
                        jnp.concatenate([dq[m, 0, pl.ds(l, QC, stride=LEAVES), :],
                                         dq[m, 1, pl.ds(l, QC, stride=LEAVES), 0:REM]], 1)
                        for m in ready], 0)
                    high = e.astype(bf16).astype(f32)
                    both = jnp.concatenate([high, e - high], 0).astype(bf16)
                    cols = slice(k * 128, (k + 1) * 128)
                    part = dot_nn(both, kh_s[i, :, cols])
                    part_l = dot_nn(both, kl_s[i, :, cols])
                    value = part[:many] + part[many:] + part_l[:many]
                    live = iota((many, PTS), 1).astype(f32) < cntb[pl.ds(l + GHOST, 1), :]
                    out[probes, lanes(l)] = jnp.where(live, near[probes, lanes(l)] + value, 0.0)
                return carry

            lax.fori_loop(0, LEAVES // 2, far, 0, unroll=2)

    scratch = [
        pltpu.VMEM((EXT, 8, 128), f32),
        pltpu.VMEM((EXT, 8, 128), f32),
        pltpu.VMEM((EXT, PROBES, PTS), f32),
        pltpu.VMEM((EXT, 128), f32),
        pltpu.VMEM((REACH, LEAVES, 128), f32),
        pltpu.VMEM((2, 8 + 2 * GHOST, 48, 128), bf16),
        pltpu.VMEM((PTS, REACH * 128), f32),
        pltpu.VMEM((PTS, REACH * 128), f32),
        pltpu.VMEM((LEAVES // 2, EQUIV, 256), bf16),
        pltpu.VMEM((LEAVES // 2, EQUIV, 256), bf16),
        pltpu.VMEM((2, PROBES * LEAVES, 128), f32),
        pltpu.VMEM((CHUNKS, LEAVES, CW), f32),
        pltpu.VMEM((CHUNKS, 3 * LEAVES, CW), bf16),
        pltpu.VMEM((CHUNKS, bits * CAP, CW), f32),
        pltpu.VMEM((CHUNKS, rows, CW), f32),
        pltpu.VMEM((2, TYPES * LEAVES, 128), f32),
        pltpu.VMEM((TYPES * LEAVES, rows), bf16),
        pltpu.VMEM((KW, EQUIV), bf16),
        pltpu.VMEM((KW, EQUIV), bf16),
        pltpu.VMEM((TYPES * EQUIV, EQUIV), f32),
        pltpu.VMEM((2 * QC * LEAVES, KW), bf16),
        pltpu.VMEM((2, 2 * QC * LEAVES, EQUIV), f32),
        pltpu.VMEM((PROBES, LEAVES * PTS), f32),
        pltpu.VMEM((CHUNKS, 2, QC * LEAVES, 128), f32),
        pltpu.VMEM((256, 256), bf16),
        pltpu.VMEM((256, 256), bf16),
        pltpu.VMEM((EQUIV, EQUIV), bf16),
        pltpu.VMEM((EQUIV, EQUIV), bf16),
        pltpu.VMEM((2, 3, GHOST * PTS), f32),
        pltpu.VMEM((2, PROBES, GHOST * PTS), f32),
        pltpu.VMEM((2, 1, LEAVES), jnp.int32),
        pltpu.VMEM((bits, bits, CAP), jnp.int32),
        pltpu.SemaphoreType.DMA((bits,)),
        pltpu.SemaphoreType.DMA((bits,)),
        pltpu.SemaphoreType.DMA((2, 3)),
        pltpu.SemaphoreType.DMA((2, 3)),
        pltpu.SemaphoreType.DMA((CHUNKS, bits)),
        pltpu.SemaphoreType.DMA((CHUNKS, bits)),
    ]
    return kern, scratch


def shards(offsets, charges, counts, u_list, v_src, v_type, wanted, m2l, uc2e, dc2e):
    count = lax.axis_size("cube")
    bits = count.bit_length() - 1
    surface = np.zeros((8, 256), np.float32)
    surface[:3, :EQUIV] = np.float32(SURFACE_RADIUS) * surface_table()
    kern, scratch = make_kernel(bits, count)
    vmem = pl.BlockSpec(memory_space=pltpu.VMEM)
    return pl.pallas_call(
        kern,
        out_shape=jax.ShapeDtypeStruct((PROBES, LEAVES * PTS), f32),
        in_specs=[vmem] * 11,
        out_specs=vmem,
        scratch_shapes=scratch,
        name="fmm_apply",
        compiler_params=pltpu.CompilerParams(
            collective_id=0, has_side_effects=True, vmem_limit_bytes=60 << 20
        ),
    )(
        offsets, charges, counts.reshape(1, LEAVES), u_list, v_src, v_type,
        wanted.reshape(bits, CAP), m2l, uc2e, dc2e, jnp.asarray(surface),
    )


def solution(mesh):
    in_specs = (
        P(None, "cube"),
        P(None, "cube"),
        P("cube"),
        P("cube", None),
        P("cube", None),
        P("cube", None),
        P("cube", None, None),
        P(),
        P(),
        P(),
    )
    out_specs = P(None, "cube")
    return jax.shard_map(shards, mesh=mesh, in_specs=in_specs, out_specs=out_specs, check_vma=False)
```

```python
import math

import jax
import jax.numpy as jnp
import numpy as np
from jax import lax
from jax.experimental import pallas as pl
from jax.experimental.pallas import tpu as pltpu
from jax.sharding import PartitionSpec as P

GHOST = 8
SOFTEN = 0.01
INV_FOUR_PI = 1.0 / (4.0 * math.pi)
SURFACE_RADIUS = 0.55

LEAVES = 32
PTS = 128
PROBES = 16
EQUIV = 152
TYPES = 16
U_SLOTS = 27
V_SLOTS = 32
CAP = 16
EXT = LEAVES + 2 * GHOST
REACH = 2 * GHOST + 1
CHUNKS = 4
QC = PROBES // CHUNKS
STARTS = (0, 2, 5)
REM = EQUIV - 128
MAIN = QC * 128
CW = MAIN + 128
REM_TILES = PROBES * REM // 128
KW = TYPES * 128 + TYPES * 32
MESH = pl.DeviceIdType.MESH
f32, bf16 = jnp.float32, jnp.bfloat16


def surface_table():
    lattice = np.arange(6)
    coords = np.stack(np.meshgrid(lattice, lattice, lattice, indexing="ij"), 0).reshape(3, -1)
    coords = (coords - 2.5) / 2.5
    on_face = np.max(np.abs(coords), axis=0) > 0.99
    return coords[:, on_face].astype(np.float32)


def dot_nt(a, b):
    return lax.dot_general(a, b, (((1,), (1,)), ((), ())), preferred_element_type=f32)


def dot_nn(a, b):
    return lax.dot_general(a, b, (((1,), (0,)), ((), ())), preferred_element_type=f32)


def split(x):
    high = x.astype(bf16)
    return high, (x - high.astype(f32)).astype(bf16)


def split3(x):
    first = x.astype(bf16).astype(f32)
    rest = x - first
    second = rest.astype(bf16).astype(f32)
    return first, second, rest - second


def iota(shape, dim):
    return lax.broadcasted_iota(jnp.int32, shape, dim)


def source_rows(x):
    row = iota(x.shape, 0)
    x = jnp.where(row < 3, x, 0.0)
    norm = jnp.sum(x * x, axis=0, keepdims=True) + SOFTEN
    e = jnp.where(row == 3, norm, jnp.where(row == 4, 1.0, x))
    a, b, c = split3(e)
    return jnp.concatenate([a, b, a, c, a, b], axis=0)


def target_rows(x):
    row = iota(x.shape, 0)
    x = jnp.where(row < 3, x, 0.0)
    norm = jnp.sum(x * x, axis=0, keepdims=True)
    e = jnp.where(row == 3, 1.0, jnp.where(row == 4, norm, -2.0 * x))
    a, b, c = split3(e)
    return jnp.concatenate([a, a, b, a, c, b], axis=0)


def column(row_vec, n, shift):
    m = row_vec.shape[1]
    wide = jnp.broadcast_to(row_vec.astype(f32), (n, m))
    hit = iota((n, m), 1) == iota((n, m), 0) + shift
    return jnp.sum(jnp.where(hit, wide, 0.0), axis=1, keepdims=True)


def lanes(i, width=128):
    return pl.ds(pl.multiple_of(i * width, width), width)


def make_kernel(bits, count):
    rows = bits * CAP + LEAVES

    def kern(off, chg, cnt, ulist, vsrc, vtype, wanted, m2l_in, uc, dc, surf, out,
             c3, pts, mq, cntb, mult, fs, dist_a, dist_b, kh_s, kl_s, chk, up, ups, stage, got, tlf, tl,
             mh, ml, turned, lm, byr, halves, near, dq, uch, ucl, dch, dcl, hoff, hchg, hcnt, wrecv,
             m2l, m_sem, w_ss, w_rs, h_ss, h_rs, d_ss, d_rs):
        me = lax.axis_index("cube")
        first = me * LEAVES
        partners = [jnp.bitwise_xor(me, 1 << b) for b in range(bits)]
        nxt = lax.rem(me + 1, count)
        prv = lax.rem(me + count - 1, count)

        barrier = pltpu.get_barrier_semaphore()
        for other in partners + [nxt, prv]:
            pl.semaphore_signal(barrier, inc=1, device_id=(other,), device_id_type=MESH)

        fetch = pltpu.make_async_copy(m2l_in, m2l, m_sem)
        fetch.start()

        ids = first - GHOST + iota((8, 128), 1)
        axis = iota((8, 128), 0)
        corner = jnp.zeros((8, 128), jnp.int32)
        for digit in range(5):
            corner = corner + ((lax.shift_right_arithmetic(ids, axis + 3 * digit) & 1) << digit)
        corner = jnp.where(axis < 3, corner, 0).astype(f32)
        for h in range(EXT):
            c3[h] = jnp.broadcast_to(corner[:, h:h + 1], (8, 128))
        lane = iota((PROBES, PTS), 1).astype(f32)
        pts[...] = jnp.zeros((EXT, 8, 128), f32)
        cntb[GHOST:GHOST + LEAVES, :] = jnp.broadcast_to(column(cnt[...], LEAVES, 0), (LEAVES, 128))

        def place(h, position, charge):
            pts[h, 0:3, :] = position + c3[h, 0:3, :]
            live = lane < cntb[pl.ds(h, 1), :]
            mq[h] = jnp.where(live, charge, 0.0) * INV_FOUR_PI

        def own_leaf(l, carry):
            place(l + GHOST, off[:, lanes(l)], chg[:, lanes(l)])
            return carry

        lax.fori_loop(0, LEAVES, own_leaf, 0, unroll=4)

        def want(b):
            return pltpu.make_async_remote_copy(
                src_ref=wanted.at[b], dst_ref=wrecv.at[b], send_sem=w_ss.at[b], recv_sem=w_rs.at[b],
                device_id=(partners[b],), device_id_type=MESH)

        def halo_copies():
            halos = []
            width = GHOST * PTS
            for side, other, begin in ((0, nxt, LEAVES * PTS - width), (1, prv, 0)):
                for k, (src, dst) in enumerate((
                        (off.at[:, pl.ds(begin, width)], hoff.at[side]),
                        (chg.at[:, pl.ds(begin, width)], hchg.at[side]),
                        (cnt, hcnt.at[side]))):
                    halos.append(pltpu.make_async_remote_copy(
                        src_ref=src, dst_ref=dst, send_sem=h_ss.at[side, k], recv_sem=h_rs.at[side, k],
                        device_id=(other,), device_id_type=MESH))
            return halos

        def greet():
            pl.semaphore_wait(barrier, bits + 2)
            for b in sorted(range(bits), key=lambda b: (b not in (3, 4), b)):
                want(b).start()
            for copy in halo_copies():
                copy.start()

        uch[...] = jnp.zeros(uch.shape, bf16)
        ucl[...] = jnp.zeros(ucl.shape, bf16)
        u_h, u_l = split(uc[...])
        uch[0:128, 0:EQUIV] = u_h[0:128]
        ucl[0:128, 0:EQUIV] = u_l[0:128]
        for g in range(4):
            uch[128 + 32 * g:128 + 32 * g + REM, 0:EQUIV] = u_h[128:EQUIV]
            ucl[128 + 32 * g:128 + 32 * g + REM, 0:EQUIV] = u_l[128:EQUIV]
        chk[1] = jnp.zeros((PROBES * LEAVES, 128), f32)
        surf_cols = jnp.transpose(source_rows(surf[...]))[:EQUIV].astype(bf16)

        def upward(j, carry):
            upward_pair(2 * j)
            upward_pair(2 * j + 1)

            @pl.when(j == 5)
            def _():
                greet()

            return carry

        def upward_pair(i):
            sides = []
            for k in range(2):
                h = 2 * i + k + GHOST
                sides.append(target_rows(pts[h] - (c3[h] + 0.5)).astype(bf16))
            tile = lax.rsqrt(dot_nn(surf_cols, jnp.concatenate(sides, 1)))
            k_h, k_l = split(tile)
            kh_s[i] = k_h
            kl_s[i] = k_l
            for k in range(2):
                l = 2 * i + k
                part = slice(k * 128, (k + 1) * 128)
                q_h, q_l = split(mq[l + GHOST])
                both = dot_nt(jnp.concatenate([q_h, q_l], 0), k_h[:, part])
                check = both[:PROBES] + both[PROBES:] + dot_nt(q_h, k_l[:, part])
                chk[0, pl.ds(l, PROBES, stride=LEAVES), :] = check[:, :128]
                chk[1, pl.ds(l, PROBES, stride=LEAVES), 0:REM] = check[:, 128:]

        lax.fori_loop(0, LEAVES // 4, upward, 0)
        c_h, c_l = split(jnp.concatenate([chk[0], chk[1]], 1))
        dens = dot_nt(c_h, uch[...]) + dot_nt(c_l, uch[...]) + dot_nt(c_h, ucl[...])
        for q in range(PROBES):
            c, qq = q // QC, q % QC
            up[c, :, qq * 128:(qq + 1) * 128] = dens[q * LEAVES:(q + 1) * LEAVES, :128]
        spots = iota((LEAVES, 128), 1)
        tails = [jnp.zeros((LEAVES, 128), f32) for _ in range(CHUNKS)]
        for q in range(PROBES):
            begin = REM * q
            moved = dens[q * LEAVES:(q + 1) * LEAVES, 128:]
            if begin % 128:
                moved = pltpu.roll(moved, begin % 128, 1)
            for m in range(begin // 128, (begin + REM - 1) // 128 + 1):
                inside = (spots >= begin - 128 * m) & (spots < begin + REM - 128 * m)
                tails[m] = jnp.where(inside, moved, tails[m])
        for c in range(CHUNKS):
            up[c, :, MAIN:] = tails[c]
        for c in range(CHUNKS):
            value = up[c]
            got[c, bits * CAP:rows, :] = value
            a, b, d = split3(value)
            ups[c] = jnp.concatenate([a, b, d], 0).astype(bf16)

        rel = ulist[...] - (first - GHOST) - iota((LEAVES, U_SLOTS), 0)
        for o in range(REACH):
            hits = jnp.sum(jnp.where(rel == o, 1.0, 0.0), axis=1, keepdims=True)
            mult[o] = jnp.broadcast_to(hits, (LEAVES, 128))

        def tally(l, carry):
            kinds = jnp.broadcast_to(vtype[pl.ds(l, 1), :], (TYPES, V_SLOTS))
            codes = jnp.broadcast_to(vsrc[pl.ds(l, 1), :], (256, V_SLOTS))
            of_kind = jnp.where(kinds == iota((TYPES, V_SLOTS), 0), 1.0, 0.0).astype(bf16)
            of_code = jnp.where(codes == iota((256, V_SLOTS), 0), 1.0, 0.0).astype(bf16)
            found = dot_nt(of_kind, of_code)
            tlf[0, pl.ds(l, TYPES, stride=LEAVES), :] = found[:, :128]
            tlf[1, pl.ds(l, TYPES, stride=LEAVES), :] = found[:, 128:]
            return carry

        lax.fori_loop(0, LEAVES, tally, 0, unroll=4)
        tl[...] = jnp.concatenate([tlf[0], tlf[1]], 1)[:, :rows].astype(bf16)

        def wide(c):
            return CW if c < REM_TILES else MAIN

        def send(c, b):
            return pltpu.make_async_remote_copy(
                src_ref=stage.at[c, pl.ds(b * CAP, CAP), pl.ds(0, wide(c))],
                dst_ref=got.at[c, pl.ds(b * CAP, CAP), pl.ds(0, wide(c))],
                send_sem=d_ss.at[c, b], recv_sem=d_rs.at[c, b],
                device_id=(partners[b],), device_id_type=MESH)

        def serve(chosen):
            picks = []
            for b in chosen:
                want(b).wait()
                listed = column(wrecv[b], CAP, 0)
                slot = (iota((CAP, 3 * LEAVES), 1) % LEAVES).astype(f32)
                picks.append(jnp.where(listed == slot, 1.0, 0.0))
            pick = jnp.concatenate(picks, 0).astype(bf16)
            for c in range(CHUNKS):
                taken = dot_nn(pick, ups[c])
                for k, b in enumerate(chosen):
                    stage[c, b * CAP:(b + 1) * CAP, :] = taken[k * CAP:(k + 1) * CAP]
            for b in chosen:
                send(0, b).start()

        far_bits = [b for b in (4,) if b < bits]
        near_bits = [b for b in (3, 2, 1, 6, 8, 5, 7, 0) if b < bits]
        order = far_bits + near_bits
        serve(near_bits)

        fetch.wait()
        for n in range(TYPES * EQUIV // 128):
            turned[n * 128:(n + 1) * 128, :] = jnp.transpose(m2l[:, n * 128:(n + 1) * 128])
        for t in range(TYPES):
            a, b = split(turned[t * EQUIV:t * EQUIV + 128, :])
            mh[t * 128:(t + 1) * 128, :] = a
            ml[t * 128:(t + 1) * 128, :] = b
            a, b = split(jnp.concatenate(
                [turned[t * EQUIV + 128:(t + 1) * EQUIV, :], jnp.zeros((32 - REM, EQUIV), f32)], 0))
            mh[TYPES * 128 + t * 32:TYPES * 128 + (t + 1) * 32, :] = a
            ml[TYPES * 128 + t * 32:TYPES * 128 + (t + 1) * 32, :] = b
        d_h, d_l = split(dc[...] * INV_FOUR_PI)
        dch[...] = d_h
        dcl[...] = d_l
        serve(far_bits)

        def block_of(l):
            return l // 8, c3[(l // 8) * 8 + GHOST] + 1.0

        def distances(l, slot, dest):
            base, middle = block_of(l)
            rows_t = jnp.transpose(target_rows(pts[l + GHOST] - middle)).astype(bf16)
            at = l - base * 8
            for o in range(0, REACH, 2):
                both = [o, o + 1] if o + 1 < REACH else [o]
                src = jnp.concatenate([fs[slot, at + k] for k in both], 1)
                dest[:, o * 128:(o + len(both)) * 128] = dot_nn(rows_t, src)

        def reduce(l, dist):
            acc = jnp.zeros((2 * PROBES, PTS), f32)
            acc_l = jnp.zeros((PROBES, PTS), f32)
            for o in range(0, REACH, 2):
                both = [o, o + 1] if o + 1 < REACH else [o]
                k_h, k_l = split(lax.rsqrt(dist[:, o * 128:(o + len(both)) * 128]))
                weighted = jnp.concatenate([mq[l + k] * mult[k, pl.ds(l, 1), :] for k in both], 1)
                w_h, w_l = split(weighted)
                acc = acc + dot_nt(jnp.concatenate([w_h, w_l], 0), k_h)
                acc_l = acc_l + dot_nt(w_h, k_l)
            near[:, lanes(l)] = acc[:PROBES] + acc[PROBES:] + acc_l

        def near_half(half, carry):
            @pl.when(half == 1)
            def _():
                for copy in halo_copies():
                    copy.wait()
                cntb[0:GHOST, :] = jnp.broadcast_to(column(hcnt[0], GHOST, LEAVES - GHOST), (GHOST, 128))
                cntb[LEAVES + GHOST:EXT, :] = jnp.broadcast_to(column(hcnt[1], GHOST, 0), (GHOST, 128))
                for side, h0 in ((0, 0), (1, LEAVES + GHOST)):
                    for k in range(GHOST):
                        place(h0 + k, hoff[side, :, k * PTS:(k + 1) * PTS],
                              hchg[side, :, k * PTS:(k + 1) * PTS])

            def leaf(i):
                return lax.rem(GHOST + half * 16 + i, LEAVES)

            def prepare(k, inner):
                for slot in range(2):
                    base = (leaf(8 * slot) // 8) * 8
                    fs[slot, k] = source_rows(pts[base + k] - (c3[base + GHOST] + 1.0)).astype(bf16)
                return inner

            lax.fori_loop(0, 8 + 2 * GHOST, prepare, 0, unroll=2)
            distances(leaf(0), 0, dist_a)

            def pair(j, inner):
                for c, when in enumerate(STARTS, 1):
                    @pl.when(half * 8 + j == when)
                    def _(c=c):
                        for b in order:
                            send(c, b).start()
                l0, l1 = leaf(2 * j), leaf(2 * j + 1)
                i2 = jnp.minimum(2 * j + 2, 15)
                distances(l1, j // 4, dist_b)
                reduce(l0, dist_a)
                distances(leaf(i2), i2 // 8, dist_a)
                reduce(l1, dist_b)
                return inner

            lax.fori_loop(0, 8, pair, 0)
            return carry

        lax.fori_loop(0, 2, near_half, 0)

        def place_tails(c):
            for g in range(QC):
                begin = REM * (c * QC + g)
                tile, at = begin // 128, begin % 128
                first_part = min(REM, 128 - at)
                for tt in range(TYPES // 4):
                    total = jnp.zeros((LEAVES, 128), f32)
                    for j in range(4):
                        leaves_t = slice((4 * tt + j) * LEAVES, (4 * tt + j + 1) * LEAVES)
                        turn = (32 * j - at) % 128
                        for m, low, high in ((tile, 0, first_part), (tile + 1, first_part, REM)):
                            if low == high:
                                continue
                            part = byr[m, leaves_t]
                            if turn:
                                part = pltpu.roll(part, turn, 1)
                            inside = (spots >= 32 * j + low) & (spots < 32 * j + high)
                            total = jnp.where(inside, part, total)
                    b_h, b_l = split(total)
                    cols = slice(TYPES * 128 + tt * 128, TYPES * 128 + (tt + 1) * 128)
                    lm[g * LEAVES:(g + 1) * LEAVES, cols] = b_h
                    lm[(QC + g) * LEAVES:(QC + g + 1) * LEAVES, cols] = b_l

        for c in range(CHUNKS):
            if c == REM_TILES:
                place_tails(c)
            for b in order:
                send(c, b).wait()
            for n in range(QC // 2):
                g_h, g_l = split(got[c, :, n * 256:(n + 1) * 256])
                upper = split(dot_nn(tl[:256], g_h) + dot_nn(tl[:256], g_l))
                lower = split(dot_nn(tl[256:], g_h) + dot_nn(tl[256:], g_l))
                for t in range(TYPES):
                    b_h, b_l = (x[(t % 8) * LEAVES:(t % 8 + 1) * LEAVES] for x in (upper, lower)[t // 8])
                    for k in range(2):
                        qq = 2 * n + k
                        r = slice(qq * LEAVES, (qq + 1) * LEAVES)
                        r2 = slice((QC + qq) * LEAVES, (QC + qq + 1) * LEAVES)
                        s = slice(t * 128, (t + 1) * 128)
                        lm[r, s] = b_h[:, k * 128:(k + 1) * 128]
                        lm[r2, s] = b_l[:, k * 128:(k + 1) * 128]
            if c < REM_TILES:
                g_h, g_l = split(got[c, :, MAIN:])
                byr[c, :256] = dot_nn(tl[:256], g_h) + dot_nn(tl[:256], g_l)
                byr[c, 256:] = dot_nn(tl[256:], g_h) + dot_nn(tl[256:], g_l)
                place_tails(c)
            half = QC * LEAVES
            cut = KW // 2
            halves[0, :] = dot_nn(lm[:, :cut], mh[:cut])
            halves[1, :] = dot_nn(lm[:, cut:], mh[cut:])
            halves[0, :half] = halves[0, :half] + dot_nn(lm[0:half, :cut], ml[:cut])
            halves[1, :half] = halves[1, :half] + dot_nn(lm[0:half, cut:], ml[cut:])
            down = (halves[0, :half] + halves[0, half:]) + (halves[1, :half] + halves[1, half:])
            w_h, w_l = split(down)
            eq = dot_nt(w_h, dch[...]) + dot_nt(w_l, dch[...]) + dot_nt(w_h, dcl[...])
            dq[c, 0] = eq[:, :128]
            dq[c, 1, :, 0:REM] = eq[:, 128:]
            if c < CHUNKS - 2:
                continue
            ready = [c] if c == CHUNKS - 1 else list(range(c + 1))
            probes = slice(ready[0] * QC, (ready[-1] + 1) * QC)
            many = len(ready) * QC

            def far(i, carry):
                rows_h, rows_l = [], []
                for k in range(2):
                    l = 2 * i + k
                    e = jnp.concatenate([
                        jnp.concatenate([dq[m, 0, pl.ds(l, QC, stride=LEAVES), :],
                                         dq[m, 1, pl.ds(l, QC, stride=LEAVES), 0:REM]], 1)
                        for m in ready], 0)
                    rows_h.append(e.astype(bf16).astype(f32))
                    rows_l.append(e - rows_h[-1])
                both = jnp.concatenate(rows_h + rows_l, 0).astype(bf16)
                part = dot_nn(both, kh_s[i])
                value = part[:2 * many] + part[2 * many:] + dot_nn(both, kl_s[i])[:2 * many]
                for k in range(2):
                    l = 2 * i + k
                    live = iota((many, PTS), 1).astype(f32) < cntb[pl.ds(l + GHOST, 1), :]
                    mine = value[k * many:(k + 1) * many, k * 128:(k + 1) * 128]
                    out[probes, lanes(l)] = jnp.where(live, near[probes, lanes(l)] + mine, 0.0)
                return carry

            lax.fori_loop(0, LEAVES // 2, far, 0, unroll=2)

    scratch = [
        pltpu.VMEM((EXT, 8, 128), f32),
        pltpu.VMEM((EXT, 8, 128), f32),
        pltpu.VMEM((EXT, PROBES, PTS), f32),
        pltpu.VMEM((EXT, 128), f32),
        pltpu.VMEM((REACH, LEAVES, 128), f32),
        pltpu.VMEM((2, 8 + 2 * GHOST, 48, 128), bf16),
        pltpu.VMEM((PTS, REACH * 128), f32),
        pltpu.VMEM((PTS, REACH * 128), f32),
        pltpu.VMEM((LEAVES // 2, EQUIV, 256), bf16),
        pltpu.VMEM((LEAVES // 2, EQUIV, 256), bf16),
        pltpu.VMEM((2, PROBES * LEAVES, 128), f32),
        pltpu.VMEM((CHUNKS, LEAVES, CW), f32),
        pltpu.VMEM((CHUNKS, 3 * LEAVES, CW), bf16),
        pltpu.VMEM((CHUNKS, bits * CAP, CW), f32),
        pltpu.VMEM((CHUNKS, rows, CW), f32),
        pltpu.VMEM((2, TYPES * LEAVES, 128), f32),
        pltpu.VMEM((TYPES * LEAVES, rows), bf16),
        pltpu.VMEM((KW, EQUIV), bf16),
        pltpu.VMEM((KW, EQUIV), bf16),
        pltpu.VMEM((TYPES * EQUIV, EQUIV), f32),
        pltpu.VMEM((2 * QC * LEAVES, KW), bf16),
        pltpu.VMEM((REM_TILES, TYPES * LEAVES, 128), f32),
        pltpu.VMEM((2, 2 * QC * LEAVES, EQUIV), f32),
        pltpu.VMEM((PROBES, LEAVES * PTS), f32),
        pltpu.VMEM((CHUNKS, 2, QC * LEAVES, 128), f32),
        pltpu.VMEM((256, 256), bf16),
        pltpu.VMEM((256, 256), bf16),
        pltpu.VMEM((EQUIV, EQUIV), bf16),
        pltpu.VMEM((EQUIV, EQUIV), bf16),
        pltpu.VMEM((2, 3, GHOST * PTS), f32),
        pltpu.VMEM((2, PROBES, GHOST * PTS), f32),
        pltpu.VMEM((2, 1, LEAVES), jnp.int32),
        pltpu.VMEM((bits, 1, CAP), jnp.int32),
        pltpu.VMEM((EQUIV, TYPES * EQUIV), f32),
        pltpu.SemaphoreType.DMA,
        pltpu.SemaphoreType.DMA((bits,)),
        pltpu.SemaphoreType.DMA((bits,)),
        pltpu.SemaphoreType.DMA((2, 3)),
        pltpu.SemaphoreType.DMA((2, 3)),
        pltpu.SemaphoreType.DMA((CHUNKS, bits)),
        pltpu.SemaphoreType.DMA((CHUNKS, bits)),
    ]
    return kern, scratch


def shards(offsets, charges, counts, u_list, v_src, v_type, wanted, m2l, uc2e, dc2e):
    count = lax.axis_size("cube")
    bits = count.bit_length() - 1
    surface = np.zeros((8, 256), np.float32)
    surface[:3, :EQUIV] = np.float32(SURFACE_RADIUS) * surface_table()
    kern, scratch = make_kernel(bits, count)
    vmem = pl.BlockSpec(memory_space=pltpu.VMEM)
    return pl.pallas_call(
        kern,
        out_shape=jax.ShapeDtypeStruct((PROBES, LEAVES * PTS), f32),
        in_specs=[vmem] * 7 + [pl.BlockSpec(memory_space=pl.ANY)] + [vmem] * 3,
        out_specs=vmem,
        scratch_shapes=scratch,
        name="fmm_apply",
        compiler_params=pltpu.CompilerParams(
            collective_id=0, has_side_effects=True, vmem_limit_bytes=28 << 20
        ),
    )(
        offsets, charges, counts.reshape(1, LEAVES), u_list, v_src, v_type,
        wanted.reshape(bits, 1, CAP), m2l, uc2e, dc2e, jnp.asarray(surface),
    )


def solution(mesh):
    in_specs = (
        P(None, "cube"),
        P(None, "cube"),
        P("cube"),
        P("cube", None),
        P("cube", None),
        P("cube", None),
        P("cube", None, None),
        P(),
        P(),
        P(),
    )
    out_specs = P(None, "cube")
    return jax.shard_map(shards, mesh=mesh, in_specs=in_specs, out_specs=out_specs, check_vma=False)
```

```python
import math

import jax
import jax.numpy as jnp
import numpy as np
from jax import lax
from jax.experimental import pallas as pl
from jax.experimental.pallas import tpu as pltpu
from jax.sharding import PartitionSpec as P

GHOST = 8
SOFTEN = 0.01
INV_FOUR_PI = 1.0 / (4.0 * math.pi)
SURFACE_RADIUS = 0.55

LEAVES = 32
PTS = 128
PROBES = 16
EQUIV = 152
TYPES = 16
U_SLOTS = 27
V_SLOTS = 32
CAP = 16
EXT = LEAVES + 2 * GHOST
REACH = 2 * GHOST + 1
CHUNKS = 4
QC = PROBES // CHUNKS
STARTS = (0, 2, 5)
REM = EQUIV - 128
MAIN = QC * 128
CW = MAIN + 128
REM_TILES = PROBES * REM // 128
KW = TYPES * 128 + TYPES * 32
MESH = pl.DeviceIdType.MESH
f32, bf16 = jnp.float32, jnp.bfloat16


def surface_table():
    lattice = np.arange(6)
    coords = np.stack(np.meshgrid(lattice, lattice, lattice, indexing="ij"), 0).reshape(3, -1)
    coords = (coords - 2.5) / 2.5
    on_face = np.max(np.abs(coords), axis=0) > 0.99
    return coords[:, on_face].astype(np.float32)


def dot_nt(a, b):
    return lax.dot_general(a, b, (((1,), (1,)), ((), ())), preferred_element_type=f32)


def dot_nn(a, b):
    return lax.dot_general(a, b, (((1,), (0,)), ((), ())), preferred_element_type=f32)


def split(x):
    high = x.astype(bf16)
    return high, (x - high.astype(f32)).astype(bf16)


def split3(x):
    first = x.astype(bf16).astype(f32)
    rest = x - first
    second = rest.astype(bf16).astype(f32)
    return first, second, rest - second


def iota(shape, dim):
    return lax.broadcasted_iota(jnp.int32, shape, dim)


def source_rows(x):
    row = iota(x.shape, 0)
    x = jnp.where(row < 3, x, 0.0)
    norm = jnp.sum(x * x, axis=0, keepdims=True) + SOFTEN
    e = jnp.where(row == 3, norm, jnp.where(row == 4, 1.0, x))
    a, b, c = split3(e)
    return jnp.concatenate([a, b, a, c, a, b], axis=0)


def target_rows(x):
    row = iota(x.shape, 0)
    x = jnp.where(row < 3, x, 0.0)
    norm = jnp.sum(x * x, axis=0, keepdims=True)
    e = jnp.where(row == 3, 1.0, jnp.where(row == 4, norm, -2.0 * x))
    a, b, c = split3(e)
    return jnp.concatenate([a, a, b, a, c, b], axis=0)


def column(row_vec, n, shift):
    m = row_vec.shape[1]
    wide = jnp.broadcast_to(row_vec.astype(f32), (n, m))
    hit = iota((n, m), 1) == iota((n, m), 0) + shift
    return jnp.sum(jnp.where(hit, wide, 0.0), axis=1, keepdims=True)


def lanes(i, width=128):
    return pl.ds(pl.multiple_of(i * width, width), width)


def make_kernel(bits, count):
    rows = bits * CAP + LEAVES

    def kern(*refs):
        (*given, out,
         off, chg, cnt, ulist, vsrc, vtype, wanted, m2l, uc, dc, surf, in_sem,
         c3, pts, mq, cntb, mult, fs, dist_a, dist_b, kh_s, kl_s, chk, up, ups, stage, got, tlf, tl,
         mh, ml, turned, lm, byr, halves, near, dq, uch, ucl, dch, dcl, hoff, hchg, hcnt, wrecv,
         w_ss, w_rs, h_ss, h_rs, d_ss, d_rs) = refs
        me = lax.axis_index("cube")
        first = me * LEAVES
        partners = [jnp.bitwise_xor(me, 1 << b) for b in range(bits)]
        nxt = lax.rem(me + 1, count)
        prv = lax.rem(me + count - 1, count)

        barrier = pltpu.get_barrier_semaphore()
        for other in partners + [nxt, prv]:
            pl.semaphore_signal(barrier, inc=1, device_id=(other,), device_id_type=MESH)

        held = (off, chg, cnt, ulist, vsrc, vtype, wanted, m2l, uc, dc, surf)
        fetches = [pltpu.make_async_copy(src, dst, in_sem.at[k]) for k, (src, dst) in enumerate(zip(given, held))]
        for k in (0, 1, 2, 8, 10, 6, 3, 4, 5, 9, 7):
            fetches[k].start()
        for k in (0, 1, 2, 8, 10, 6, 3, 4, 5, 9):
            fetches[k].wait()

        ids = first - GHOST + iota((8, 128), 1)
        axis = iota((8, 128), 0)
        corner = jnp.zeros((8, 128), jnp.int32)
        for digit in range(5):
            corner = corner + ((lax.shift_right_arithmetic(ids, axis + 3 * digit) & 1) << digit)
        corner = jnp.where(axis < 3, corner, 0).astype(f32)
        for h in range(EXT):
            c3[h] = jnp.broadcast_to(corner[:, h:h + 1], (8, 128))
        lane = iota((PROBES, PTS), 1).astype(f32)
        pts[...] = jnp.zeros((EXT, 8, 128), f32)
        cntb[GHOST:GHOST + LEAVES, :] = jnp.broadcast_to(column(cnt[...], LEAVES, 0), (LEAVES, 128))

        def place(h, position, charge):
            pts[h, 0:3, :] = position + c3[h, 0:3, :]
            live = lane < cntb[pl.ds(h, 1), :]
            mq[h] = jnp.where(live, charge, 0.0) * INV_FOUR_PI

        def own_leaf(l, carry):
            place(l + GHOST, off[:, lanes(l)], chg[:, lanes(l)])
            return carry

        lax.fori_loop(0, LEAVES, own_leaf, 0, unroll=4)

        def want(b):
            return pltpu.make_async_remote_copy(
                src_ref=wanted.at[b], dst_ref=wrecv.at[b], send_sem=w_ss.at[b], recv_sem=w_rs.at[b],
                device_id=(partners[b],), device_id_type=MESH)

        def halo_copies():
            halos = []
            width = GHOST * PTS
            for side, other, begin in ((0, nxt, LEAVES * PTS - width), (1, prv, 0)):
                for k, (src, dst) in enumerate((
                        (off.at[:, pl.ds(begin, width)], hoff.at[side]),
                        (chg.at[:, pl.ds(begin, width)], hchg.at[side]),
                        (cnt, hcnt.at[side]))):
                    halos.append(pltpu.make_async_remote_copy(
                        src_ref=src, dst_ref=dst, send_sem=h_ss.at[side, k], recv_sem=h_rs.at[side, k],
                        device_id=(other,), device_id_type=MESH))
            return halos

        def greet():
            pl.semaphore_wait(barrier, bits + 2)
            for b in sorted(range(bits), key=lambda b: (b not in (3, 4), b)):
                want(b).start()
            for copy in halo_copies():
                copy.start()

        uch[...] = jnp.zeros(uch.shape, bf16)
        ucl[...] = jnp.zeros(ucl.shape, bf16)
        u_h, u_l = split(uc[...])
        uch[0:128, 0:EQUIV] = u_h[0:128]
        ucl[0:128, 0:EQUIV] = u_l[0:128]
        for g in range(4):
            uch[128 + 32 * g:128 + 32 * g + REM, 0:EQUIV] = u_h[128:EQUIV]
            ucl[128 + 32 * g:128 + 32 * g + REM, 0:EQUIV] = u_l[128:EQUIV]
        chk[1] = jnp.zeros((PROBES * LEAVES, 128), f32)
        surf_cols = jnp.transpose(source_rows(surf[...]))[:EQUIV].astype(bf16)

        def upward(j, carry):
            upward_pair(2 * j)
            upward_pair(2 * j + 1)

            @pl.when(j == 5)
            def _():
                greet()

            return carry

        def upward_pair(i):
            sides = []
            for k in range(2):
                h = 2 * i + k + GHOST
                sides.append(target_rows(pts[h] - (c3[h] + 0.5)).astype(bf16))
            tile = lax.rsqrt(dot_nn(surf_cols, jnp.concatenate(sides, 1)))
            k_h, k_l = split(tile)
            kh_s[i] = k_h
            kl_s[i] = k_l
            for k in range(2):
                l = 2 * i + k
                part = slice(k * 128, (k + 1) * 128)
                q_h, q_l = split(mq[l + GHOST])
                both = dot_nt(jnp.concatenate([q_h, q_l], 0), k_h[:, part])
                check = both[:PROBES] + both[PROBES:] + dot_nt(q_h, k_l[:, part])
                chk[0, pl.ds(l, PROBES, stride=LEAVES), :] = check[:, :128]
                chk[1, pl.ds(l, PROBES, stride=LEAVES), 0:REM] = check[:, 128:]

        lax.fori_loop(0, LEAVES // 4, upward, 0)
        c_h, c_l = split(jnp.concatenate([chk[0], chk[1]], 1))
        dens = dot_nt(c_h, uch[...]) + dot_nt(c_l, uch[...]) + dot_nt(c_h, ucl[...])
        for q in range(PROBES):
            c, qq = q // QC, q % QC
            up[c, :, qq * 128:(qq + 1) * 128] = dens[q * LEAVES:(q + 1) * LEAVES, :128]
        spots = iota((LEAVES, 128), 1)
        tails = [jnp.zeros((LEAVES, 128), f32) for _ in range(CHUNKS)]
        for q in range(PROBES):
            begin = REM * q
            moved = dens[q * LEAVES:(q + 1) * LEAVES, 128:]
            if begin % 128:
                moved = pltpu.roll(moved, begin % 128, 1)
            for m in range(begin // 128, (begin + REM - 1) // 128 + 1):
                inside = (spots >= begin - 128 * m) & (spots < begin + REM - 128 * m)
                tails[m] = jnp.where(inside, moved, tails[m])
        for c in range(CHUNKS):
            up[c, :, MAIN:] = tails[c]
        for c in range(CHUNKS):
            value = up[c]
            got[c, bits * CAP:rows, :] = value
            a, b, d = split3(value)
            ups[c] = jnp.concatenate([a, b, d], 0).astype(bf16)

        rel = ulist[...] - (first - GHOST) - iota((LEAVES, U_SLOTS), 0)
        for o in range(REACH):
            hits = jnp.sum(jnp.where(rel == o, 1.0, 0.0), axis=1, keepdims=True)
            mult[o] = jnp.broadcast_to(hits, (LEAVES, 128))

        def tally(l, carry):
            kinds = jnp.broadcast_to(vtype[pl.ds(l, 1), :], (TYPES, V_SLOTS))
            codes = jnp.broadcast_to(vsrc[pl.ds(l, 1), :], (256, V_SLOTS))
            of_kind = jnp.where(kinds == iota((TYPES, V_SLOTS), 0), 1.0, 0.0).astype(bf16)
            of_code = jnp.where(codes == iota((256, V_SLOTS), 0), 1.0, 0.0).astype(bf16)
            found = dot_nt(of_kind, of_code)
            tlf[0, pl.ds(l, TYPES, stride=LEAVES), :] = found[:, :128]
            tlf[1, pl.ds(l, TYPES, stride=LEAVES), :] = found[:, 128:]
            return carry

        lax.fori_loop(0, LEAVES, tally, 0, unroll=4)
        tl[...] = jnp.concatenate([tlf[0], tlf[1]], 1)[:, :rows].astype(bf16)

        def wide(c):
            return CW if c < REM_TILES else MAIN

        def send(c, b):
            return pltpu.make_async_remote_copy(
                src_ref=stage.at[c, pl.ds(b * CAP, CAP), pl.ds(0, wide(c))],
                dst_ref=got.at[c, pl.ds(b * CAP, CAP), pl.ds(0, wide(c))],
                send_sem=d_ss.at[c, b], recv_sem=d_rs.at[c, b],
                device_id=(partners[b],), device_id_type=MESH)

        def serve(chosen):
            picks = []
            for b in chosen:
                want(b).wait()
                listed = column(wrecv[b], CAP, 0)
                slot = (iota((CAP, 3 * LEAVES), 1) % LEAVES).astype(f32)
                picks.append(jnp.where(listed == slot, 1.0, 0.0))
            pick = jnp.concatenate(picks, 0).astype(bf16)
            for c in range(CHUNKS):
                taken = dot_nn(pick, ups[c])
                for k, b in enumerate(chosen):
                    stage[c, b * CAP:(b + 1) * CAP, :] = taken[k * CAP:(k + 1) * CAP]
            for b in chosen:
                send(0, b).start()

        far_bits = [b for b in (4,) if b < bits]
        near_bits = [b for b in (3, 2, 1, 6, 8, 5, 7, 0) if b < bits]
        order = far_bits + near_bits
        serve(near_bits)

        fetches[7].wait()
        for n in range(TYPES * EQUIV // 128):
            turned[n * 128:(n + 1) * 128, :] = jnp.transpose(m2l[:, n * 128:(n + 1) * 128])
        for t in range(TYPES):
            a, b = split(turned[t * EQUIV:t * EQUIV + 128, :])
            mh[t * 128:(t + 1) * 128, :] = a
            ml[t * 128:(t + 1) * 128, :] = b
            a, b = split(jnp.concatenate(
                [turned[t * EQUIV + 128:(t + 1) * EQUIV, :], jnp.zeros((32 - REM, EQUIV), f32)], 0))
            mh[TYPES * 128 + t * 32:TYPES * 128 + (t + 1) * 32, :] = a
            ml[TYPES * 128 + t * 32:TYPES * 128 + (t + 1) * 32, :] = b
        d_h, d_l = split(dc[...] * INV_FOUR_PI)
        dch[...] = d_h
        dcl[...] = d_l
        serve(far_bits)

        def block_of(l):
            return l // 8, c3[(l // 8) * 8 + GHOST] + 1.0

        def distances(l, slot, dest):
            base, middle = block_of(l)
            rows_t = jnp.transpose(target_rows(pts[l + GHOST] - middle)).astype(bf16)
            at = l - base * 8
            for o in range(0, REACH, 2):
                both = [o, o + 1] if o + 1 < REACH else [o]
                src = jnp.concatenate([fs[slot, at + k] for k in both], 1)
                dest[:, o * 128:(o + len(both)) * 128] = dot_nn(rows_t, src)

        def reduce(l, dist):
            acc = jnp.zeros((2 * PROBES, PTS), f32)
            acc_l = jnp.zeros((PROBES, PTS), f32)
            for o in range(0, REACH, 2):
                both = [o, o + 1] if o + 1 < REACH else [o]
                k_h, k_l = split(lax.rsqrt(dist[:, o * 128:(o + len(both)) * 128]))
                weighted = jnp.concatenate([mq[l + k] * mult[k, pl.ds(l, 1), :] for k in both], 1)
                w_h, w_l = split(weighted)
                acc = acc + dot_nt(jnp.concatenate([w_h, w_l], 0), k_h)
                acc_l = acc_l + dot_nt(w_h, k_l)
            near[:, lanes(l)] = acc[:PROBES] + acc[PROBES:] + acc_l

        def near_half(half, carry):
            @pl.when(half == 1)
            def _():
                for copy in halo_copies():
                    copy.wait()
                cntb[0:GHOST, :] = jnp.broadcast_to(column(hcnt[0], GHOST, LEAVES - GHOST), (GHOST, 128))
                cntb[LEAVES + GHOST:EXT, :] = jnp.broadcast_to(column(hcnt[1], GHOST, 0), (GHOST, 128))
                for side, h0 in ((0, 0), (1, LEAVES + GHOST)):
                    for k in range(GHOST):
                        place(h0 + k, hoff[side, :, k * PTS:(k + 1) * PTS],
                              hchg[side, :, k * PTS:(k + 1) * PTS])

            def leaf(i):
                return lax.rem(GHOST + half * 16 + i, LEAVES)

            def prepare(k, inner):
                for slot in range(2):
                    base = (leaf(8 * slot) // 8) * 8
                    fs[slot, k] = source_rows(pts[base + k] - (c3[base + GHOST] + 1.0)).astype(bf16)
                return inner

            lax.fori_loop(0, 8 + 2 * GHOST, prepare, 0, unroll=2)
            distances(leaf(0), 0, dist_a)

            def pair(j, inner):
                for c, when in enumerate(STARTS, 1):
                    @pl.when(half * 8 + j == when)
                    def _(c=c):
                        for b in order:
                            send(c, b).start()
                l0, l1 = leaf(2 * j), leaf(2 * j + 1)
                i2 = jnp.minimum(2 * j + 2, 15)
                distances(l1, j // 4, dist_b)
                reduce(l0, dist_a)
                distances(leaf(i2), i2 // 8, dist_a)
                reduce(l1, dist_b)
                return inner

            lax.fori_loop(0, 8, pair, 0)
            return carry

        lax.fori_loop(0, 2, near_half, 0)

        def place_tails(c):
            for g in range(QC):
                begin = REM * (c * QC + g)
                tile, at = begin // 128, begin % 128
                first_part = min(REM, 128 - at)
                for tt in range(TYPES // 4):
                    total = jnp.zeros((LEAVES, 128), f32)
                    for j in range(4):
                        leaves_t = slice((4 * tt + j) * LEAVES, (4 * tt + j + 1) * LEAVES)
                        turn = (32 * j - at) % 128
                        for m, low, high in ((tile, 0, first_part), (tile + 1, first_part, REM)):
                            if low == high:
                                continue
                            part = byr[m, leaves_t]
                            if turn:
                                part = pltpu.roll(part, turn, 1)
                            inside = (spots >= 32 * j + low) & (spots < 32 * j + high)
                            total = jnp.where(inside, part, total)
                    b_h, b_l = split(total)
                    cols = slice(TYPES * 128 + tt * 128, TYPES * 128 + (tt + 1) * 128)
                    lm[g * LEAVES:(g + 1) * LEAVES, cols] = b_h
                    lm[(QC + g) * LEAVES:(QC + g + 1) * LEAVES, cols] = b_l

        for c in range(CHUNKS):
            if c == REM_TILES:
                place_tails(c)
            for b in order:
                send(c, b).wait()
            for n in range(QC // 2):
                g_h, g_l = split(got[c, :, n * 256:(n + 1) * 256])
                upper = split(dot_nn(tl[:256], g_h) + dot_nn(tl[:256], g_l))
                lower = split(dot_nn(tl[256:], g_h) + dot_nn(tl[256:], g_l))
                for t in range(TYPES):
                    b_h, b_l = (x[(t % 8) * LEAVES:(t % 8 + 1) * LEAVES] for x in (upper, lower)[t // 8])
                    for k in range(2):
                        qq = 2 * n + k
                        r = slice(qq * LEAVES, (qq + 1) * LEAVES)
                        r2 = slice((QC + qq) * LEAVES, (QC + qq + 1) * LEAVES)
                        s = slice(t * 128, (t + 1) * 128)
                        lm[r, s] = b_h[:, k * 128:(k + 1) * 128]
                        lm[r2, s] = b_l[:, k * 128:(k + 1) * 128]
            if c < REM_TILES:
                g_h, g_l = split(got[c, :, MAIN:])
                byr[c, :256] = dot_nn(tl[:256], g_h) + dot_nn(tl[:256], g_l)
                byr[c, 256:] = dot_nn(tl[256:], g_h) + dot_nn(tl[256:], g_l)
                place_tails(c)
            half = QC * LEAVES
            cut = KW // 2
            halves[0, :] = dot_nn(lm[:, :cut], mh[:cut])
            halves[1, :] = dot_nn(lm[:, cut:], mh[cut:])
            halves[0, :half] = halves[0, :half] + dot_nn(lm[0:half, :cut], ml[:cut])
            halves[1, :half] = halves[1, :half] + dot_nn(lm[0:half, cut:], ml[cut:])
            down = (halves[0, :half] + halves[0, half:]) + (halves[1, :half] + halves[1, half:])
            w_h, w_l = split(down)
            eq = dot_nt(w_h, dch[...]) + dot_nt(w_l, dch[...]) + dot_nt(w_h, dcl[...])
            dq[c, 0] = eq[:, :128]
            dq[c, 1, :, 0:REM] = eq[:, 128:]
            if c < CHUNKS - 2:
                continue
            ready = [c] if c == CHUNKS - 1 else list(range(c + 1))
            probes = slice(ready[0] * QC, (ready[-1] + 1) * QC)
            many = len(ready) * QC

            def far(i, carry):
                rows_h, rows_l = [], []
                for k in range(2):
                    l = 2 * i + k
                    e = jnp.concatenate([
                        jnp.concatenate([dq[m, 0, pl.ds(l, QC, stride=LEAVES), :],
                                         dq[m, 1, pl.ds(l, QC, stride=LEAVES), 0:REM]], 1)
                        for m in ready], 0)
                    rows_h.append(e.astype(bf16).astype(f32))
                    rows_l.append(e - rows_h[-1])
                both = jnp.concatenate(rows_h + rows_l, 0).astype(bf16)
                part = dot_nn(both, kh_s[i])
                value = part[:2 * many] + part[2 * many:] + dot_nn(both, kl_s[i])[:2 * many]
                for k in range(2):
                    l = 2 * i + k
                    live = iota((many, PTS), 1).astype(f32) < cntb[pl.ds(l + GHOST, 1), :]
                    mine = value[k * many:(k + 1) * many, k * 128:(k + 1) * 128]
                    out[probes, lanes(l)] = jnp.where(live, near[probes, lanes(l)] + mine, 0.0)
                return carry

            lax.fori_loop(0, LEAVES // 2, far, 0, unroll=2)

    scratch = [
        pltpu.VMEM((3, LEAVES * PTS), f32),
        pltpu.VMEM((PROBES, LEAVES * PTS), f32),
        pltpu.VMEM((1, LEAVES), jnp.int32),
        pltpu.VMEM((LEAVES, U_SLOTS), jnp.int32),
        pltpu.VMEM((LEAVES, V_SLOTS), jnp.int32),
        pltpu.VMEM((LEAVES, V_SLOTS), jnp.int32),
        pltpu.VMEM((bits, 1, CAP), jnp.int32),
        pltpu.VMEM((EQUIV, TYPES * EQUIV), f32),
        pltpu.VMEM((EQUIV, EQUIV), f32),
        pltpu.VMEM((EQUIV, EQUIV), f32),
        pltpu.VMEM((8, 256), f32),
        pltpu.SemaphoreType.DMA((11,)),
        pltpu.VMEM((EXT, 8, 128), f32),
        pltpu.VMEM((EXT, 8, 128), f32),
        pltpu.VMEM((EXT, PROBES, PTS), f32),
        pltpu.VMEM((EXT, 128), f32),
        pltpu.VMEM((REACH, LEAVES, 128), f32),
        pltpu.VMEM((2, 8 + 2 * GHOST, 48, 128), bf16),
        pltpu.VMEM((PTS, REACH * 128), f32),
        pltpu.VMEM((PTS, REACH * 128), f32),
        pltpu.VMEM((LEAVES // 2, EQUIV, 256), bf16),
        pltpu.VMEM((LEAVES // 2, EQUIV, 256), bf16),
        pltpu.VMEM((2, PROBES * LEAVES, 128), f32),
        pltpu.VMEM((CHUNKS, LEAVES, CW), f32),
        pltpu.VMEM((CHUNKS, 3 * LEAVES, CW), bf16),
        pltpu.VMEM((CHUNKS, bits * CAP, CW), f32),
        pltpu.VMEM((CHUNKS, rows, CW), f32),
        pltpu.VMEM((2, TYPES * LEAVES, 128), f32),
        pltpu.VMEM((TYPES * LEAVES, rows), bf16),
        pltpu.VMEM((KW, EQUIV), bf16),
        pltpu.VMEM((KW, EQUIV), bf16),
        pltpu.VMEM((TYPES * EQUIV, EQUIV), f32),
        pltpu.VMEM((2 * QC * LEAVES, KW), bf16),
        pltpu.VMEM((REM_TILES, TYPES * LEAVES, 128), f32),
        pltpu.VMEM((2, 2 * QC * LEAVES, EQUIV), f32),
        pltpu.VMEM((PROBES, LEAVES * PTS), f32),
        pltpu.VMEM((CHUNKS, 2, QC * LEAVES, 128), f32),
        pltpu.VMEM((256, 256), bf16),
        pltpu.VMEM((256, 256), bf16),
        pltpu.VMEM((EQUIV, EQUIV), bf16),
        pltpu.VMEM((EQUIV, EQUIV), bf16),
        pltpu.VMEM((2, 3, GHOST * PTS), f32),
        pltpu.VMEM((2, PROBES, GHOST * PTS), f32),
        pltpu.VMEM((2, 1, LEAVES), jnp.int32),
        pltpu.VMEM((bits, 1, CAP), jnp.int32),
        pltpu.SemaphoreType.DMA((bits,)),
        pltpu.SemaphoreType.DMA((bits,)),
        pltpu.SemaphoreType.DMA((2, 3)),
        pltpu.SemaphoreType.DMA((2, 3)),
        pltpu.SemaphoreType.DMA((CHUNKS, bits)),
        pltpu.SemaphoreType.DMA((CHUNKS, bits)),
    ]
    return kern, scratch


def shards(offsets, charges, counts, u_list, v_src, v_type, wanted, m2l, uc2e, dc2e):
    count = lax.axis_size("cube")
    bits = count.bit_length() - 1
    surface = np.zeros((8, 256), np.float32)
    surface[:3, :EQUIV] = np.float32(SURFACE_RADIUS) * surface_table()
    kern, scratch = make_kernel(bits, count)
    vmem = pl.BlockSpec(memory_space=pltpu.VMEM)
    return pl.pallas_call(
        kern,
        out_shape=jax.ShapeDtypeStruct((PROBES, LEAVES * PTS), f32),
        in_specs=[pl.BlockSpec(memory_space=pltpu.HBM)] * 11,
        out_specs=vmem,
        scratch_shapes=scratch,
        name="fmm_apply",
        compiler_params=pltpu.CompilerParams(
            collective_id=0, has_side_effects=True, vmem_limit_bytes=60 << 20
        ),
    )(
        offsets, charges, counts.reshape(1, LEAVES), u_list, v_src, v_type,
        wanted.reshape(bits, 1, CAP), m2l, uc2e, dc2e, jnp.asarray(surface),
    )


def solution(mesh):
    in_specs = (
        P(None, "cube"),
        P(None, "cube"),
        P("cube"),
        P("cube", None),
        P("cube", None),
        P("cube", None),
        P("cube", None, None),
        P(),
        P(),
        P(),
    )
    out_specs = P(None, "cube")
    return jax.shard_map(shards, mesh=mesh, in_specs=in_specs, out_specs=out_specs, check_vma=False)
```

```python
import math

import jax
import jax.numpy as jnp
import numpy as np
from jax import lax
from jax.experimental import pallas as pl
from jax.experimental.pallas import tpu as pltpu
from jax.sharding import PartitionSpec as P

GHOST = 8
SOFTEN = 0.01
INV_FOUR_PI = 1.0 / (4.0 * math.pi)
SURFACE_RADIUS = 0.55

LEAVES = 32
PTS = 128
PROBES = 16
EQUIV = 152
TYPES = 16
U_SLOTS = 27
V_SLOTS = 32
CAP = 16
EXT = LEAVES + 2 * GHOST
REACH = 2 * GHOST + 1
CHUNKS = 4
QC = PROBES // CHUNKS
STARTS = (0, 2, 5)
REM = EQUIV - 128
MAIN = QC * 128
CW = MAIN + 128
REM_TILES = PROBES * REM // 128
KW = TYPES * 128 + TYPES * 32
MESH = pl.DeviceIdType.MESH
f32, bf16 = jnp.float32, jnp.bfloat16


def surface_table():
    lattice = np.arange(6)
    coords = np.stack(np.meshgrid(lattice, lattice, lattice, indexing="ij"), 0).reshape(3, -1)
    coords = (coords - 2.5) / 2.5
    on_face = np.max(np.abs(coords), axis=0) > 0.99
    return coords[:, on_face].astype(np.float32)


def dot_nt(a, b):
    return lax.dot_general(a, b, (((1,), (1,)), ((), ())), preferred_element_type=f32)


def dot_nn(a, b):
    return lax.dot_general(a, b, (((1,), (0,)), ((), ())), preferred_element_type=f32)


def split(x):
    high = x.astype(bf16)
    return high, (x - high.astype(f32)).astype(bf16)


def split3(x):
    first = x.astype(bf16).astype(f32)
    rest = x - first
    second = rest.astype(bf16).astype(f32)
    return first, second, rest - second


def iota(shape, dim):
    return lax.broadcasted_iota(jnp.int32, shape, dim)


def source_rows(x):
    row = iota(x.shape, 0)
    x = jnp.where(row < 3, x, 0.0)
    norm = jnp.sum(x * x, axis=0, keepdims=True) + SOFTEN
    e = jnp.where(row == 3, norm, jnp.where(row == 4, 1.0, x))
    a, b, c = split3(e)
    return jnp.concatenate([a, b, a, c, a, b], axis=0)


def target_rows(x):
    row = iota(x.shape, 0)
    x = jnp.where(row < 3, x, 0.0)
    norm = jnp.sum(x * x, axis=0, keepdims=True)
    e = jnp.where(row == 3, 1.0, jnp.where(row == 4, norm, -2.0 * x))
    a, b, c = split3(e)
    return jnp.concatenate([a, a, b, a, c, b], axis=0)


def column(row_vec, n, shift):
    m = row_vec.shape[1]
    wide = jnp.broadcast_to(row_vec.astype(f32), (n, m))
    hit = iota((n, m), 1) == iota((n, m), 0) + shift
    return jnp.sum(jnp.where(hit, wide, 0.0), axis=1, keepdims=True)


def lanes(i, width=128):
    return pl.ds(pl.multiple_of(i * width, width), width)


def make_kernel(bits, count):
    rows = bits * CAP + LEAVES

    def kern(*refs):
        (*given, out,
         off, chg, cnt, ulist, vsrc, vtype, wanted, m2l, uc, dc, surf, in_sem,
         c3, pts, mq, cntb, mult, fs, dist_a, dist_b, kh_s, kl_s, chk, up, ups, stage, got, tlf, tl,
         mh, ml, turned, lm, byr, halves, near, dq, uch, ucl, dch, dcl, hoff, hchg, hcnt, wrecv,
         w_ss, w_rs, h_ss, h_rs, d_ss, d_rs) = refs
        me = lax.axis_index("cube")
        first = me * LEAVES
        partners = [jnp.bitwise_xor(me, 1 << b) for b in range(bits)]
        nxt = lax.rem(me + 1, count)
        prv = lax.rem(me + count - 1, count)

        barrier = pltpu.get_barrier_semaphore()
        for other in partners + [nxt, prv]:
            pl.semaphore_signal(barrier, inc=1, device_id=(other,), device_id_type=MESH)

        held = (off, chg, cnt, ulist, vsrc, vtype, wanted, m2l, uc, dc, surf)
        fetches = [pltpu.make_async_copy(src, dst, in_sem.at[k]) for k, (src, dst) in enumerate(zip(given, held))]
        for k in (0, 1, 2, 8, 10, 6, 3, 4, 5, 9, 7):
            fetches[k].start()
        for k in (0, 1, 2, 8, 10, 6, 3, 4, 5, 9):
            fetches[k].wait()

        ids = first - GHOST + iota((8, 128), 1)
        axis = iota((8, 128), 0)
        corner = jnp.zeros((8, 128), jnp.int32)
        for digit in range(5):
            corner = corner + ((lax.shift_right_arithmetic(ids, axis + 3 * digit) & 1) << digit)
        corner = jnp.where(axis < 3, corner, 0).astype(f32)
        for h in range(EXT):
            c3[h] = jnp.broadcast_to(corner[:, h:h + 1], (8, 128))
        lane = iota((PROBES, PTS), 1).astype(f32)
        pts[...] = jnp.zeros((EXT, 8, 128), f32)
        cntb[GHOST:GHOST + LEAVES, :] = jnp.broadcast_to(column(cnt[...], LEAVES, 0), (LEAVES, 128))

        def place(h, position, charge):
            pts[h, 0:3, :] = position + c3[h, 0:3, :]
            live = lane < cntb[pl.ds(h, 1), :]
            mq[h] = jnp.where(live, charge, 0.0) * INV_FOUR_PI

        def own_leaf(l, carry):
            place(l + GHOST, off[:, lanes(l)], chg[:, lanes(l)])
            return carry

        lax.fori_loop(0, LEAVES, own_leaf, 0, unroll=4)

        def want(b):
            return pltpu.make_async_remote_copy(
                src_ref=wanted.at[b], dst_ref=wrecv.at[b], send_sem=w_ss.at[b], recv_sem=w_rs.at[b],
                device_id=(partners[b],), device_id_type=MESH)

        def halo_copies():
            halos = []
            width = GHOST * PTS
            for side, other, begin in ((0, nxt, LEAVES * PTS - width), (1, prv, 0)):
                for k, (src, dst) in enumerate((
                        (off.at[:, pl.ds(begin, width)], hoff.at[side]),
                        (chg.at[:, pl.ds(begin, width)], hchg.at[side]),
                        (cnt, hcnt.at[side]))):
                    halos.append(pltpu.make_async_remote_copy(
                        src_ref=src, dst_ref=dst, send_sem=h_ss.at[side, k], recv_sem=h_rs.at[side, k],
                        device_id=(other,), device_id_type=MESH))
            return halos

        def greet():
            pl.semaphore_wait(barrier, bits + 2)
            for b in sorted(range(bits), key=lambda b: (b not in (3, 4), b)):
                want(b).start()
            for copy in halo_copies():
                copy.start()

        uch[...] = jnp.zeros(uch.shape, bf16)
        ucl[...] = jnp.zeros(ucl.shape, bf16)
        u_h, u_l = split(uc[...])
        uch[0:128, 0:EQUIV] = u_h[0:128]
        ucl[0:128, 0:EQUIV] = u_l[0:128]
        for g in range(4):
            uch[128 + 32 * g:128 + 32 * g + REM, 0:EQUIV] = u_h[128:EQUIV]
            ucl[128 + 32 * g:128 + 32 * g + REM, 0:EQUIV] = u_l[128:EQUIV]
        chk[1] = jnp.zeros((PROBES * LEAVES, 128), f32)
        surf_cols = jnp.transpose(source_rows(surf[...]))[:EQUIV].astype(bf16)

        def upward(j, carry):
            upward_pair(2 * j)
            upward_pair(2 * j + 1)

            @pl.when(j == 5)
            def _():
                greet()

            return carry

        def upward_pair(i):
            sides = []
            for k in range(2):
                h = 2 * i + k + GHOST
                sides.append(target_rows(pts[h] - (c3[h] + 0.5)).astype(bf16))
            tile = lax.rsqrt(dot_nn(surf_cols, jnp.concatenate(sides, 1)))
            k_h, k_l = split(tile)
            kh_s[i] = k_h
            kl_s[i] = k_l
            for k in range(2):
                l = 2 * i + k
                part = slice(k * 128, (k + 1) * 128)
                q_h, q_l = split(mq[l + GHOST])
                both = dot_nt(jnp.concatenate([q_h, q_l], 0), k_h[:, part])
                check = both[:PROBES] + both[PROBES:] + dot_nt(q_h, k_l[:, part])
                chk[0, pl.ds(l, PROBES, stride=LEAVES), :] = check[:, :128]
                chk[1, pl.ds(l, PROBES, stride=LEAVES), 0:REM] = check[:, 128:]

        lax.fori_loop(0, LEAVES // 4, upward, 0)
        c_h, c_l = split(jnp.concatenate([chk[0], chk[1]], 1))
        dens = dot_nt(c_h, uch[...]) + dot_nt(c_l, uch[...]) + dot_nt(c_h, ucl[...])
        for q in range(PROBES):
            c, qq = q // QC, q % QC
            up[c, :, qq * 128:(qq + 1) * 128] = dens[q * LEAVES:(q + 1) * LEAVES, :128]
        spots = iota((LEAVES, 128), 1)
        tails = [jnp.zeros((LEAVES, 128), f32) for _ in range(CHUNKS)]
        for q in range(PROBES):
            begin = REM * q
            moved = dens[q * LEAVES:(q + 1) * LEAVES, 128:]
            if begin % 128:
                moved = pltpu.roll(moved, begin % 128, 1)
            for m in range(begin // 128, (begin + REM - 1) // 128 + 1):
                inside = (spots >= begin - 128 * m) & (spots < begin + REM - 128 * m)
                tails[m] = jnp.where(inside, moved, tails[m])
        for c in range(CHUNKS):
            up[c, :, MAIN:] = tails[c]
        for c in range(CHUNKS):
            value = up[c]
            got[c, bits * CAP:rows, :] = value
            a, b, d = split3(value)
            ups[c] = jnp.concatenate([a, b, d], 0).astype(bf16)

        rel = ulist[...] - (first - GHOST) - iota((LEAVES, U_SLOTS), 0)
        for o in range(REACH):
            hits = jnp.sum(jnp.where(rel == o, 1.0, 0.0), axis=1, keepdims=True)
            mult[o] = jnp.broadcast_to(hits, (LEAVES, 128))

        def tally(l, carry):
            kinds = jnp.broadcast_to(vtype[pl.ds(l, 1), :], (TYPES, V_SLOTS))
            codes = jnp.broadcast_to(vsrc[pl.ds(l, 1), :], (256, V_SLOTS))
            of_kind = jnp.where(kinds == iota((TYPES, V_SLOTS), 0), 1.0, 0.0).astype(bf16)
            of_code = jnp.where(codes == iota((256, V_SLOTS), 0), 1.0, 0.0).astype(bf16)
            found = dot_nt(of_kind, of_code)
            tlf[0, pl.ds(l, TYPES, stride=LEAVES), :] = found[:, :128]
            tlf[1, pl.ds(l, TYPES, stride=LEAVES), :] = found[:, 128:]
            return carry

        lax.fori_loop(0, LEAVES, tally, 0, unroll=4)
        tl[...] = jnp.concatenate([tlf[0], tlf[1]], 1)[:, :rows].astype(bf16)

        def wide(c):
            return CW if c < REM_TILES else MAIN

        def send(c, b):
            return pltpu.make_async_remote_copy(
                src_ref=stage.at[c, pl.ds(b * CAP, CAP), pl.ds(0, wide(c))],
                dst_ref=got.at[c, pl.ds(b * CAP, CAP), pl.ds(0, wide(c))],
                send_sem=d_ss.at[c, b], recv_sem=d_rs.at[c, b],
                device_id=(partners[b],), device_id_type=MESH)

        def serve(chosen):
            picks = []
            for b in chosen:
                want(b).wait()
                listed = column(wrecv[b], CAP, 0)
                slot = (iota((CAP, 3 * LEAVES), 1) % LEAVES).astype(f32)
                picks.append(jnp.where(listed == slot, 1.0, 0.0))
            pick = jnp.concatenate(picks, 0).astype(bf16)
            for c in range(CHUNKS):
                taken = dot_nn(pick, ups[c])
                for k, b in enumerate(chosen):
                    stage[c, b * CAP:(b + 1) * CAP, :] = taken[k * CAP:(k + 1) * CAP]
            for b in chosen:
                send(0, b).start()

        def leaf_at(half, i):
            return lax.rem(GHOST + half * 16 + i, LEAVES)

        def prepare_half(half):
            def prepare(k, inner):
                for slot in range(2):
                    base = (leaf_at(half, 8 * slot) // 8) * 8
                    local = pts[base + k] - (c3[base + GHOST] + 1.0)
                    fs[slot, k] = jnp.transpose(source_rows(local)).astype(bf16)
                return inner

            lax.fori_loop(0, 8 + 2 * GHOST, prepare, 0, unroll=2)

        prepare_half(0)
        far_bits = [b for b in (4,) if b < bits]
        near_bits = [b for b in (3, 2, 1, 6, 8, 5, 7, 0) if b < bits]
        order = far_bits + near_bits
        serve(near_bits)

        fetches[7].wait()
        for n in range(TYPES * EQUIV // 128):
            turned[n * 128:(n + 1) * 128, :] = jnp.transpose(m2l[:, n * 128:(n + 1) * 128])
        for t in range(TYPES):
            a, b = split(turned[t * EQUIV:t * EQUIV + 128, :])
            mh[t * 128:(t + 1) * 128, :] = a
            ml[t * 128:(t + 1) * 128, :] = b
            a, b = split(jnp.concatenate(
                [turned[t * EQUIV + 128:(t + 1) * EQUIV, :], jnp.zeros((32 - REM, EQUIV), f32)], 0))
            mh[TYPES * 128 + t * 32:TYPES * 128 + (t + 1) * 32, :] = a
            ml[TYPES * 128 + t * 32:TYPES * 128 + (t + 1) * 32, :] = b
        d_h, d_l = split(dc[...] * INV_FOUR_PI)
        dch[...] = d_h
        dcl[...] = d_l
        serve(far_bits)

        def block_of(l):
            return l // 8, c3[(l // 8) * 8 + GHOST] + 1.0

        def distances(l, slot, dest):
            base, middle = block_of(l)
            rows_t = target_rows(pts[l + GHOST] - middle).astype(bf16)
            at = l - base * 8
            for o in range(0, REACH, 2):
                both = [o, o + 1] if o + 1 < REACH else [o]
                src = jnp.concatenate([fs[slot, at + k] for k in both], 0)
                dest[o * 128:(o + len(both)) * 128, :] = dot_nn(src, rows_t)

        def reduce(l, dist):
            acc = jnp.zeros((2 * PROBES, PTS), f32)
            acc_l = jnp.zeros((PROBES, PTS), f32)
            for o in range(0, REACH, 2):
                both = [o, o + 1] if o + 1 < REACH else [o]
                k_h, k_l = split(lax.rsqrt(dist[o * 128:(o + len(both)) * 128, :]))
                weighted = jnp.concatenate([mq[l + k] * mult[k, pl.ds(l, 1), :] for k in both], 1)
                w_h, w_l = split(weighted)
                acc = acc + dot_nn(jnp.concatenate([w_h, w_l], 0), k_h)
                acc_l = acc_l + dot_nn(w_h, k_l)
            near[:, lanes(l)] = acc[:PROBES] + acc[PROBES:] + acc_l

        def near_half(half, carry):
            @pl.when(half == 1)
            def _():
                for copy in halo_copies():
                    copy.wait()
                cntb[0:GHOST, :] = jnp.broadcast_to(column(hcnt[0], GHOST, LEAVES - GHOST), (GHOST, 128))
                cntb[LEAVES + GHOST:EXT, :] = jnp.broadcast_to(column(hcnt[1], GHOST, 0), (GHOST, 128))
                for side, h0 in ((0, 0), (1, LEAVES + GHOST)):
                    for k in range(GHOST):
                        place(h0 + k, hoff[side, :, k * PTS:(k + 1) * PTS],
                              hchg[side, :, k * PTS:(k + 1) * PTS])
                prepare_half(1)

            def leaf(i):
                return leaf_at(half, i)

            distances(leaf(0), 0, dist_a)

            def pair(j, inner):
                for c, when in enumerate(STARTS, 1):
                    @pl.when(half * 8 + j == when)
                    def _(c=c):
                        for b in order:
                            send(c, b).start()
                l0, l1 = leaf(2 * j), leaf(2 * j + 1)
                i2 = jnp.minimum(2 * j + 2, 15)
                distances(l1, j // 4, dist_b)
                reduce(l0, dist_a)
                distances(leaf(i2), i2 // 8, dist_a)
                reduce(l1, dist_b)
                return inner

            lax.fori_loop(0, 8, pair, 0)
            return carry

        lax.fori_loop(0, 2, near_half, 0)

        def place_tails(c):
            for g in range(QC):
                begin = REM * (c * QC + g)
                tile, at = begin // 128, begin % 128
                first_part = min(REM, 128 - at)
                for tt in range(TYPES // 4):
                    total = jnp.zeros((LEAVES, 128), f32)
                    for j in range(4):
                        leaves_t = slice((4 * tt + j) * LEAVES, (4 * tt + j + 1) * LEAVES)
                        turn = (32 * j - at) % 128
                        for m, low, high in ((tile, 0, first_part), (tile + 1, first_part, REM)):
                            if low == high:
                                continue
                            part = byr[m, leaves_t]
                            if turn:
                                part = pltpu.roll(part, turn, 1)
                            inside = (spots >= 32 * j + low) & (spots < 32 * j + high)
                            total = jnp.where(inside, part, total)
                    b_h, b_l = split(total)
                    cols = slice(TYPES * 128 + tt * 128, TYPES * 128 + (tt + 1) * 128)
                    lm[g * LEAVES:(g + 1) * LEAVES, cols] = b_h
                    lm[(QC + g) * LEAVES:(QC + g + 1) * LEAVES, cols] = b_l

        for c in range(CHUNKS):
            if c == REM_TILES:
                place_tails(c)
            for b in order:
                send(c, b).wait()
            for n in range(QC // 2):
                g_h, g_l = split(got[c, :, n * 256:(n + 1) * 256])
                upper = split(dot_nn(tl[:256], g_h) + dot_nn(tl[:256], g_l))
                lower = split(dot_nn(tl[256:], g_h) + dot_nn(tl[256:], g_l))
                for t in range(TYPES):
                    b_h, b_l = (x[(t % 8) * LEAVES:(t % 8 + 1) * LEAVES] for x in (upper, lower)[t // 8])
                    for k in range(2):
                        qq = 2 * n + k
                        r = slice(qq * LEAVES, (qq + 1) * LEAVES)
                        r2 = slice((QC + qq) * LEAVES, (QC + qq + 1) * LEAVES)
                        s = slice(t * 128, (t + 1) * 128)
                        lm[r, s] = b_h[:, k * 128:(k + 1) * 128]
                        lm[r2, s] = b_l[:, k * 128:(k + 1) * 128]
            if c < REM_TILES:
                g_h, g_l = split(got[c, :, MAIN:])
                byr[c, :256] = dot_nn(tl[:256], g_h) + dot_nn(tl[:256], g_l)
                byr[c, 256:] = dot_nn(tl[256:], g_h) + dot_nn(tl[256:], g_l)
                place_tails(c)
            half = QC * LEAVES
            cut = KW // 2
            halves[0, :] = dot_nn(lm[:, :cut], mh[:cut])
            halves[1, :] = dot_nn(lm[:, cut:], mh[cut:])
            halves[0, :half] = halves[0, :half] + dot_nn(lm[0:half, :cut], ml[:cut])
            halves[1, :half] = halves[1, :half] + dot_nn(lm[0:half, cut:], ml[cut:])
            down = (halves[0, :half] + halves[0, half:]) + (halves[1, :half] + halves[1, half:])
            w_h, w_l = split(down)
            eq = dot_nt(w_h, dch[...]) + dot_nt(w_l, dch[...]) + dot_nt(w_h, dcl[...])
            dq[c, 0] = eq[:, :128]
            dq[c, 1, :, 0:REM] = eq[:, 128:]
            if c < CHUNKS - 2:
                continue
            ready = [c] if c == CHUNKS - 1 else list(range(c + 1))
            probes = slice(ready[0] * QC, (ready[-1] + 1) * QC)
            many = len(ready) * QC

            def far(i, carry):
                rows_h, rows_l = [], []
                for k in range(2):
                    l = 2 * i + k
                    e = jnp.concatenate([
                        jnp.concatenate([dq[m, 0, pl.ds(l, QC, stride=LEAVES), :],
                                         dq[m, 1, pl.ds(l, QC, stride=LEAVES), 0:REM]], 1)
                        for m in ready], 0)
                    rows_h.append(e.astype(bf16).astype(f32))
                    rows_l.append(e - rows_h[-1])
                both = jnp.concatenate(rows_h + rows_l, 0).astype(bf16)
                part = dot_nn(both, kh_s[i])
                value = part[:2 * many] + part[2 * many:] + dot_nn(both, kl_s[i])[:2 * many]
                for k in range(2):
                    l = 2 * i + k
                    live = iota((many, PTS), 1).astype(f32) < cntb[pl.ds(l + GHOST, 1), :]
                    mine = value[k * many:(k + 1) * many, k * 128:(k + 1) * 128]
                    out[probes, lanes(l)] = jnp.where(live, near[probes, lanes(l)] + mine, 0.0)
                return carry

            lax.fori_loop(0, LEAVES // 2, far, 0, unroll=2)

    scratch = [
        pltpu.VMEM((3, LEAVES * PTS), f32),
        pltpu.VMEM((PROBES, LEAVES * PTS), f32),
        pltpu.VMEM((1, LEAVES), jnp.int32),
        pltpu.VMEM((LEAVES, U_SLOTS), jnp.int32),
        pltpu.VMEM((LEAVES, V_SLOTS), jnp.int32),
        pltpu.VMEM((LEAVES, V_SLOTS), jnp.int32),
        pltpu.VMEM((bits, 1, CAP), jnp.int32),
        pltpu.VMEM((EQUIV, TYPES * EQUIV), f32),
        pltpu.VMEM((EQUIV, EQUIV), f32),
        pltpu.VMEM((EQUIV, EQUIV), f32),
        pltpu.VMEM((8, 256), f32),
        pltpu.SemaphoreType.DMA((11,)),
        pltpu.VMEM((EXT, 8, 128), f32),
        pltpu.VMEM((EXT, 8, 128), f32),
        pltpu.VMEM((EXT, PROBES, PTS), f32),
        pltpu.VMEM((EXT, 128), f32),
        pltpu.VMEM((REACH, LEAVES, 128), f32),
        pltpu.VMEM((2, 8 + 2 * GHOST, 128, 48), bf16),
        pltpu.VMEM((REACH * 128, PTS), f32),
        pltpu.VMEM((REACH * 128, PTS), f32),
        pltpu.VMEM((LEAVES // 2, EQUIV, 256), bf16),
        pltpu.VMEM((LEAVES // 2, EQUIV, 256), bf16),
        pltpu.VMEM((2, PROBES * LEAVES, 128), f32),
        pltpu.VMEM((CHUNKS, LEAVES, CW), f32),
        pltpu.VMEM((CHUNKS, 3 * LEAVES, CW), bf16),
        pltpu.VMEM((CHUNKS, bits * CAP, CW), f32),
        pltpu.VMEM((CHUNKS, rows, CW), f32),
        pltpu.VMEM((2, TYPES * LEAVES, 128), f32),
        pltpu.VMEM((TYPES * LEAVES, rows), bf16),
        pltpu.VMEM((KW, EQUIV), bf16),
        pltpu.VMEM((KW, EQUIV), bf16),
        pltpu.VMEM((TYPES * EQUIV, EQUIV), f32),
        pltpu.VMEM((2 * QC * LEAVES, KW), bf16),
        pltpu.VMEM((REM_TILES, TYPES * LEAVES, 128), f32),
        pltpu.VMEM((2, 2 * QC * LEAVES, EQUIV), f32),
        pltpu.VMEM((PROBES, LEAVES * PTS), f32),
        pltpu.VMEM((CHUNKS, 2, QC * LEAVES, 128), f32),
        pltpu.VMEM((256, 256), bf16),
        pltpu.VMEM((256, 256), bf16),
        pltpu.VMEM((EQUIV, EQUIV), bf16),
        pltpu.VMEM((EQUIV, EQUIV), bf16),
        pltpu.VMEM((2, 3, GHOST * PTS), f32),
        pltpu.VMEM((2, PROBES, GHOST * PTS), f32),
        pltpu.VMEM((2, 1, LEAVES), jnp.int32),
        pltpu.VMEM((bits, 1, CAP), jnp.int32),
        pltpu.SemaphoreType.DMA((bits,)),
        pltpu.SemaphoreType.DMA((bits,)),
        pltpu.SemaphoreType.DMA((2, 3)),
        pltpu.SemaphoreType.DMA((2, 3)),
        pltpu.SemaphoreType.DMA((CHUNKS, bits)),
        pltpu.SemaphoreType.DMA((CHUNKS, bits)),
    ]
    return kern, scratch


def shards(offsets, charges, counts, u_list, v_src, v_type, wanted, m2l, uc2e, dc2e):
    count = lax.axis_size("cube")
    bits = count.bit_length() - 1
    surface = np.zeros((8, 256), np.float32)
    surface[:3, :EQUIV] = np.float32(SURFACE_RADIUS) * surface_table()
    kern, scratch = make_kernel(bits, count)
    vmem = pl.BlockSpec(memory_space=pltpu.VMEM)
    return pl.pallas_call(
        kern,
        out_shape=jax.ShapeDtypeStruct((PROBES, LEAVES * PTS), f32),
        in_specs=[pl.BlockSpec(memory_space=pltpu.HBM)] * 11,
        out_specs=vmem,
        scratch_shapes=scratch,
        name="fmm_apply",
        compiler_params=pltpu.CompilerParams(
            collective_id=0, has_side_effects=True, vmem_limit_bytes=60 << 20
        ),
    )(
        offsets, charges, counts.reshape(1, LEAVES), u_list, v_src, v_type,
        wanted.reshape(bits, 1, CAP), m2l, uc2e, dc2e, jnp.asarray(surface),
    )


def solution(mesh):
    in_specs = (
        P(None, "cube"),
        P(None, "cube"),
        P("cube"),
        P("cube", None),
        P("cube", None),
        P("cube", None),
        P("cube", None, None),
        P(),
        P(),
        P(),
    )
    out_specs = P(None, "cube")
    return jax.shard_map(shards, mesh=mesh, in_specs=in_specs, out_specs=out_specs, check_vma=False)
```
